128 devices in a mesh: grp: 4 (over x), dev: 32 (over z, y, core).
Axes of the slice: x: 4, y: 4, z: 4, core: 2. Of those that a mesh axis runs over, the one named last changes fastest.
Arguments:
- image_tokens: bfloat16 [512, 197, 768], P(('grp', 'dev')), may hold values from -64 to 64
- text_tokens: bfloat16 [512, 30, 768], P(('grp', 'dev')), may hold values from -64 to 64
- negatives: int32 [512, 2], P(('grp', 'dev')), may hold values from 0 to 127, as said below
- query_weight: bfloat16 [768, 768], replicated, may hold values from -0.21875 to 0.21875
- kv_weight: bfloat16 [768, 1536], replicated, may hold values from -0.21875 to 0.21875
- match_head: float32 [768], replicated, may hold values from -6 to 6
- cotangent: bfloat16 [512, 3], P(('grp', 'dev')), may hold values from -6 to 6
Outputs:
- logits: float32 [512, 3], P(('grp', 'dev'))
- grad_query_weight: float32 [768, 768], P(('grp', 'dev'))
- grad_kv_weight: float32 [768, 1536], P(('grp', 'dev'))
The draws below stay inside these ranges and needn't reach their ends.
Inputs may be any that keep to these rules, and one draw needn't show every extreme that they name: At most 2 of the 8 negatives of one device lie on any one device of its group, and in every group some device holds exactly 2 negatives of every device of the group.
All inputs are finite; a program needn't handle non-finite values.
Results may differ from the reference program's by a relative error of at most 0.0085.
The reference program's roundings to bfloat16 on the way count: a program that leaves them out, or rounds other values in their place, can miss the bound.
Values may be sent and summed in bfloat16 or wider, within the bound.
No kernel may reach another device: no remote copies, remote signals or barrier semaphores. Data moves between devices by JAX's collectives and lax.ppermute only.
A program may use at most 128 MiB of HBM per device.

```python
import jax
import jax.numpy as jnp
from jax import lax

D = 768
HEADS = 12
LI = 197
LT = 30
PAIR_DEV = 4
TEXTS = 512
N_GRP = 4
N_DEV = 32


def token_rows(key, count, length):
    shape = (count, length, D)
    values = jnp.clip(jax.random.normal(jax.random.fold_in(key, 5), shape, jnp.float32), -6.0, 6.0)
    return values


def draw_image_tokens(key, part):
    return token_rows(jax.random.fold_in(key, 101), PAIR_DEV * N_GRP * N_DEV, LI).astype(jnp.bfloat16)


def draw_text_tokens(key, part):
    return token_rows(jax.random.fold_in(key, 202), PAIR_DEV * N_GRP * N_DEV, LT).astype(jnp.bfloat16)


def draw_negatives(key, part):
    capacity = max(2, (2 * PAIR_DEV + N_DEV - 1) // N_DEV)
    requests = 2 * PAIR_DEV

    def one_block(block_key, popular):
        others = (popular + 1 + jnp.tile(jnp.arange(N_DEV - 1, dtype=jnp.int32), capacity)) % N_DEV
        spread = jax.random.permutation(jax.random.fold_in(block_key, 1), others)[:requests - capacity]
        owners = jnp.concatenate([jnp.full((capacity,), popular, jnp.int32), spread])
        owners = jax.random.permutation(jax.random.fold_in(block_key, 2), owners)
        inner = jax.random.randint(jax.random.fold_in(block_key, 3), (requests,), 0, PAIR_DEV, dtype=jnp.int32)
        return (owners * PAIR_DEV + inner).reshape(PAIR_DEV, 2)
    popular_owner = jax.random.randint(jax.random.fold_in(key, 7), (N_GRP,), 0, N_DEV, dtype=jnp.int32)
    block_keys = jax.random.split(jax.random.fold_in(key, 11), N_GRP * N_DEV)
    populars = jnp.repeat(popular_owner, N_DEV)
    blocks = jax.vmap(one_block)(block_keys, populars)
    return blocks.reshape(-1, 2)


def shard_levels(own_key, extent, cuts, low, top_value):
    def one(dim, blocks):
        steps = jax.random.uniform(jax.random.fold_in(jax.random.fold_in(own_key, 6), dim), (blocks,), jnp.float32, low / len(cuts), top_value / len(cuts))
        return jnp.repeat(jnp.exp(steps), extent[dim] // blocks).reshape((-1,) + (1,) * (len(extent) - dim - 1))

    factor_of = one(*cuts[0])
    for cut in cuts[1:]:
        factor_of = factor_of * one(*cut)
    return factor_of


def scatter_about(stream_key, dims, deviation, most, pieces=(), kind=jnp.bfloat16):
    values = jax.random.normal(stream_key, dims, jnp.float32) * deviation
    if len(pieces) > 0:
        values = shard_levels(stream_key, dims, pieces, -0.22, 0.18) * values
    return jnp.clip(values, min=-most, max=most).astype(kind)


def setup_inputs(seed: int = 0) -> dict:
    streams_of = jax.random.split(jax.random.key(seed), 8)
    image_tokens = draw_image_tokens(jax.random.fold_in(streams_of[7], 71), 0)
    text_tokens = draw_text_tokens(jax.random.fold_in(streams_of[7], 71), 0)
    negatives = draw_negatives(jax.random.fold_in(streams_of[7], 71), 0)
    query_weight = scatter_about(streams_of[3], (D, D), D ** -0.5, 0.21875)
    kv_weight = scatter_about(streams_of[4], (D, 2 * D), D ** -0.5, 0.21875)
    match_head = scatter_about(streams_of[5], (D,), 1.0, 6.0, (), jnp.float32)
    cotangent = scatter_about(streams_of[6], (TEXTS, 3), 1.0, 6.0, ((0, 128),))
    return {"image_tokens": image_tokens, "text_tokens": text_tokens, "negatives": negatives, "query_weight": query_weight, "kv_weight": kv_weight, "match_head": match_head, "cotangent": cotangent}


def attend(queries, keys_values, tangent, match_head):
    count = queries.shape[0]
    text_len = queries.shape[1]
    image_len = keys_values.shape[1]
    model = queries.shape[2]
    head_size = model // HEADS
    factor = head_size ** -0.5
    query_heads = queries.astype(jnp.float32).reshape(count, text_len, HEADS, head_size)
    key_heads = keys_values[..., :model].astype(jnp.float32).reshape(count, image_len, HEADS, head_size)
    value_heads = keys_values[..., model:].astype(jnp.float32).reshape(count, image_len, HEADS, head_size)
    scores = jnp.einsum("bqhd,bkhd->bhqk", query_heads, key_heads, precision=lax.Precision.HIGHEST) * factor
    probs = jax.nn.softmax(scores, axis=-1)
    probs_low = probs.astype(jnp.bfloat16).astype(jnp.float32)
    context = jnp.einsum("bhqk,bkhd->bqhd", probs_low, value_heads, precision=lax.Precision.HIGHEST)
    pooled = jnp.mean(context, axis=1).reshape(count, model)
    logits = jnp.sum(pooled * match_head[None, :], axis=-1)
    direction = (tangent / text_len)[:, None] * match_head[None, :]
    dir_heads = direction.reshape(count, HEADS, head_size)
    d_probs = jnp.einsum("bkhd,bhd->bhk", value_heads, dir_heads, precision=lax.Precision.HIGHEST)
    d_scores = probs * (d_probs[:, :, None, :] - jnp.sum(probs * d_probs[:, :, None, :], axis=-1, keepdims=True))
    d_low = d_scores.astype(jnp.bfloat16).astype(jnp.float32)
    d_keys = jnp.einsum("bhqk,bqhd->bkhd", d_low, query_heads, precision=lax.Precision.HIGHEST) * factor
    d_queries = jnp.einsum("bhqk,bkhd->bqhd", d_low, key_heads, precision=lax.Precision.HIGHEST) * factor
    weight_sum = jnp.sum(probs_low, axis=2)
    d_values = jnp.transpose(weight_sum[..., None] * dir_heads[:, :, None, :], (0, 2, 1, 3))
    kv_grad = jnp.concatenate([d_keys.reshape(count, image_len, model), d_values.reshape(count, image_len, model)], axis=-1)
    return logits, kv_grad, d_queries.reshape(count, text_len, model)


def reference(image_tokens, text_tokens, negatives, query_weight, kv_weight, match_head, cotangent):
    text_count = text_tokens.shape[0]
    group_size = PAIR_DEV * N_DEV
    queries = jnp.dot(text_tokens.reshape(-1, D), query_weight, preferred_element_type=jnp.float32).astype(jnp.bfloat16).reshape(text_count, LT, D)
    keys_values = jnp.dot(image_tokens.reshape(-1, D), kv_weight, preferred_element_type=jnp.float32).astype(jnp.bfloat16).reshape(-1, LI, 2 * D)
    position = jnp.arange(text_count, dtype=jnp.int32)
    offset = (position // group_size) * group_size
    chosen = jnp.concatenate([position[:, None], offset[:, None] + negatives.astype(jnp.int32)], axis=1)

    def one_text(carry, item):
        grad_query, grad_kv = carry
        picks, text_query, text_rows, tangent = item
        pictures = image_tokens[picks]
        chosen_kv = keys_values[picks]
        repeated = jnp.broadcast_to(text_query[None], (3, LT, D))
        logit_row, kv_grad, query_grad = attend(repeated, chosen_kv, tangent.astype(jnp.float32), match_head)
        kv_low = kv_grad.astype(jnp.bfloat16).reshape(-1, 2 * D)
        grad_kv = grad_kv + jnp.dot(pictures.reshape(-1, D).T, kv_low, preferred_element_type=jnp.float32)
        total_query = jnp.sum(query_grad, axis=0).astype(jnp.bfloat16)
        grad_query = grad_query + jnp.dot(text_rows.T, total_query, preferred_element_type=jnp.float32)
        return (grad_query, grad_kv), logit_row

    start = (jnp.zeros((D, D), jnp.float32), jnp.zeros((D, 2 * D), jnp.float32))
    (grad_query_weight, grad_kv_weight), logits = lax.scan(one_text, start, (chosen, queries, text_tokens, cotangent))
    return logits, grad_query_weight, grad_kv_weight
```

```python
import functools

import jax
import jax.numpy as jnp
from jax import lax
from jax.experimental import pallas as pl
from jax.experimental.pallas import tpu as pltpu
from jax.sharding import Mesh
from jax.sharding import PartitionSpec as P

DEV = ("dev_0", "dev_1", "dev_2")
GRP_DEV = ("grp", "dev_0", "dev_1", "dev_2")
RINGS = ("grp", "dev_0", "dev_1")
ORDERS = ((0, 1, 2), (1, 2, 0), (2, 0, 1))

D = 768
HEADS = 12
LI = 197
LP = 200
LX = 256
LT = 30
QP = 32
GROUPS = 3
GW = 256
ROWS = 128
F32 = jnp.float32
BF16 = jnp.bfloat16


def nn(a, b):
    return lax.dot_general(a, b, (((1,), (0,)), ((), ())), preferred_element_type=F32)


def nt(a, b):
    return lax.dot_general(a, b, (((1,), (1,)), ((), ())), preferred_element_type=F32)


def tn(a, b):
    return lax.dot_general(a, b, (((0,), (0,)), ((), ())), preferred_element_type=F32)


def block_mask():
    row = lax.broadcasted_iota(jnp.int32, (ROWS, GW), 0)
    col = lax.broadcasted_iota(jnp.int32, (ROWS, GW), 1)
    return row, (row // QP) == (col // 64)


def fill_constants(head_ref, mhx_ref, ones_ref):
    row, same = block_mask()
    ones_ref[...] = jnp.where(same & (row % QP < LT), 1.0, 0.0).astype(BF16)
    for g in range(GROUPS):
        rest = head_ref[:, g * GW : (g + 1) * GW]
        for piece in range(3):
            part = rest.astype(BF16)
            rest = rest - part.astype(F32)
            wide = jnp.broadcast_to(part.astype(F32), (ROWS, GW))
            mhx_ref[piece * GROUPS + g] = jnp.where(same, wide, 0.0).astype(BF16)


def attend_pair(i, text, scale, keyval, qx_ref, head_ref, mhx_ref, ones_ref, dkv_ref, dq_ref, lrow_ref):
    tail = lax.broadcasted_iota(jnp.int32, (8, ROWS), 0) < (LI - (LP - 8))
    base = pl.multiple_of(i * LX, LX)
    trow = pl.multiple_of(text * QP, QP)
    total = jnp.zeros((1, GW), F32)
    for g in range(GROUPS):
        lo = g * GW
        keys = keyval(lo)
        values = keyval(D + lo)
        query = qx_ref[text * GROUPS + g]
        head = head_ref[:, lo : lo + GW]
        scores = nt(keys, query)
        scores = jnp.concatenate(
            [scores[: LP - 8], jnp.where(tail, scores[LP - 8 :], -1e30)], axis=0
        )
        top = jnp.max(scores, axis=0, keepdims=True)
        expd = jnp.exp(scores - top)
        probs = expd * (1.0 / jnp.sum(expd, axis=0, keepdims=True))
        probs_low = probs.astype(BF16)
        dp = nt(values, mhx_ref[g]) + nt(values, mhx_ref[GROUPS + g]) + nt(values, mhx_ref[2 * GROUPS + g])
        dp = dp * scale
        mean = jnp.sum(probs * dp, axis=0, keepdims=True)
        d_low = (probs * (dp - mean)).astype(BF16)
        dkv_ref[pl.ds(base, LP), lo : lo + GW] = nn(d_low, query).astype(BF16)
        weight = nn(probs_low, ones_ref[...])
        dkv_ref[pl.ds(base, LP), D + lo : D + lo + GW] = (weight * (head * scale)).astype(BF16)
        total = total + jnp.sum(weight * values.astype(F32), axis=0, keepdims=True) * head
        wide = tn(d_low, keys)
        col = lax.broadcasted_iota(jnp.int32, (QP, GW), 1) // 64
        dq = jnp.where(col == 0, wide[:QP], 0.0)
        for h in range(1, 4):
            dq = jnp.where(col == h, wide[h * QP : (h + 1) * QP], dq)
        dq_ref[pl.ds(trow, QP), lo : lo + GW] += dq * 0.125
    lrow_ref[pl.ds(i, 1), :] = total


def own_kernel(
    tan_ref, text_ref, qw_ref, image_ref, kvw_ref, head_ref,
    qx_ref, grad_ref, dq_ref, lrow_ref,
    mhx_ref, ones_ref, kv_ref, dkv_ref, xt_ref,
    *, pairs,
):
    fill_constants(head_ref, mhx_ref, ones_ref)
    dq_ref[...] = jnp.zeros_like(dq_ref)
    dkv_ref[...] = jnp.zeros_like(dkv_ref)
    queries = (nn(text_ref[...], qw_ref[...]).astype(BF16).astype(F32) * 0.125)
    _, same = block_mask()
    for t in range(pairs):
        for g in range(GROUPS):
            part = queries[t * QP : (t + 1) * QP, g * GW : (g + 1) * GW]
            wide = jnp.concatenate([part] * 4, axis=0)
            qx_ref[t * GROUPS + g] = jnp.where(same, wide, 0.0).astype(BF16)

    def one(i, carry):
        image = image_ref[i]
        kv_ref[...] = nn(image, kvw_ref[...]).astype(BF16)
        wide = jnp.concatenate([image, jnp.zeros((LX - LP, D), BF16)], axis=0)
        xt_ref[:, pl.ds(pl.multiple_of(i * LX, LX), LX)] = wide.T
        attend_pair(
            i, i, tan_ref[i], lambda lo: kv_ref[:, lo : lo + GW],
            qx_ref, head_ref, mhx_ref, ones_ref, dkv_ref, dq_ref, lrow_ref,
        )
        return carry

    lax.fori_loop(0, pairs, one, 0)

    def block(n, carry):
        cols = pl.ds(pl.multiple_of(n * GW, GW), GW)
        grad_ref[:, cols] = nn(xt_ref[...], dkv_ref[:, cols])
        return carry

    lax.fori_loop(0, 2 * D // GW, block, 0)


def strip_rows(color, rings):
    strips = []
    size = D // (rings[0] * rings[1] * rings[2] * 2)
    for a in range(rings[0]):
        for b in range(rings[1]):
            for c in range(rings[2]):
                at = (a, b, c)
                order = ORDERS[color]
                place = 0
                for ring in order:
                    place = place * rings[ring] + at[ring]
                for core in range(2):
                    source = (((a * rings[1] + b) * rings[2] + c) * 2 + core) * size
                    strips.append((core, source, place * size))
    return size, strips


def negatives_kernel(
    pick_ref, tan_ref, core_ref, text_ref, qx_ref, kvw_ref, head_ref, dq_in_ref, gathered_ref, grad_in_ref,
    mine_ref, other_ref, lrow_ref,
    mhx_ref, ones_ref, kv_ref, dkv_ref, xt_ref, image_ref, grad_ref, prior_ref, dq_ref, out_ref, sems, prior_sem, out_sems,
    *, pairs, rings,
):
    def fetch(i):
        return pltpu.make_async_copy(gathered_ref.at[pick_ref[i]], image_ref.at[i], sems.at[i])

    for i in range(pairs):
        fetch(i).start()
    prior = pltpu.make_async_copy(grad_in_ref, prior_ref, prior_sem)
    prior.start()
    fill_constants(head_ref, mhx_ref, ones_ref)
    dq_ref[...] = dq_in_ref[...]
    dkv_ref[...] = jnp.zeros_like(dkv_ref)

    def one(i, carry):
        fetch(i).wait()
        image = image_ref[i]
        kv_ref[...] = nn(image, kvw_ref[...]).astype(BF16)
        wide = jnp.concatenate([image, jnp.zeros((LX - LP, D), BF16)], axis=0)
        xt_ref[:, pl.ds(pl.multiple_of(i * LX, LX), LX)] = wide.T
        attend_pair(
            i, i // 2, tan_ref[i], lambda lo: kv_ref[:, lo : lo + GW],
            qx_ref, head_ref, mhx_ref, ones_ref, dkv_ref, dq_ref, lrow_ref,
        )
        return carry

    lax.fori_loop(0, pairs, one, 0)
    core = core_ref[0]
    half = D // 2

    def spread(color):
        size, strips = strip_rows(color, rings)
        for which, source, target in strips:
            slot = jnp.where(core == which, 0, 1)
            out_ref[slot, color * half + target : color * half + target + size, :] = grad_ref[
                source : source + size, :
            ]
        copies = []
        for slot, ref in ((1, other_ref), (0, mine_ref)):
            copy = pltpu.make_async_copy(
                out_ref.at[slot, pl.ds(color * half, half)],
                ref.at[pl.ds(color * half, half)],
                out_sems.at[2 * color + slot],
            )
            copy.start()
            copies.append(copy)
        return copies

    grad_ref[...] = tn(text_ref[...], dq_ref[...].astype(BF16))
    copies = spread(0)
    prior.wait()
    for part in range(2):
        def block(n, carry):
            cols = pl.ds(pl.multiple_of(n * GW, GW), GW)
            wide = pl.ds(pl.multiple_of(part * D + n * GW, GW), GW)
            grad_ref[:, cols] = nn(xt_ref[...], dkv_ref[:, wide]) + prior_ref[:, wide]
            return carry

        lax.fori_loop(0, D // GW, block, 0)
        copies += spread(part + 1)
    for copy in copies:
        copy.wait()


VM = pl.BlockSpec(memory_space=pltpu.VMEM)
SM = pl.BlockSpec(memory_space=pltpu.SMEM)
ANY = pl.BlockSpec(memory_space=pl.ANY)
LIMIT = 60 * 1024 * 1024


def own_pairs(tangent, text, query_weight, images, kv_weight, head):
    pairs = images.shape[0]
    return pl.pallas_call(
        functools.partial(own_kernel, pairs=pairs),
        name="own_pairs",
        in_specs=[SM] + [VM] * 5,
        out_specs=[VM] * 4,
        out_shape=[
            jax.ShapeDtypeStruct((pairs * GROUPS, ROWS, GW), BF16),
            jax.ShapeDtypeStruct((D, 2 * D), F32),
            jax.ShapeDtypeStruct((pairs * QP, D), F32),
            jax.ShapeDtypeStruct((pairs, GW), F32),
        ],
        scratch_shapes=[
            pltpu.VMEM((3 * GROUPS, ROWS, GW), BF16),
            pltpu.VMEM((ROWS, GW), BF16),
            pltpu.VMEM((LP, 2 * D), BF16),
            pltpu.VMEM((pairs * LX, 2 * D), BF16),
            pltpu.VMEM((D, pairs * LX), BF16),
        ],
        compiler_params=pltpu.CompilerParams(vmem_limit_bytes=LIMIT),
    )(tangent, text, query_weight, images, kv_weight, head)


def negative_pairs(picks, tangent, core, text, qx, kv_weight, head, dq, gathered, grad, rings):
    pairs = picks.shape[0]
    return pl.pallas_call(
        functools.partial(negatives_kernel, pairs=pairs, rings=rings),
        name="negative_pairs",
        in_specs=[SM] * 3 + [VM] * 5 + [ANY] * 2,
        out_specs=[ANY, ANY, VM],
        out_shape=[
            jax.ShapeDtypeStruct((3 * D // 2, D), F32),
            jax.ShapeDtypeStruct((3 * D // 2, D), F32),
            jax.ShapeDtypeStruct((pairs, GW), F32),
        ],
        scratch_shapes=[
            pltpu.VMEM((3 * GROUPS, ROWS, GW), BF16),
            pltpu.VMEM((ROWS, GW), BF16),
            pltpu.VMEM((LP, 2 * D), BF16),
            pltpu.VMEM((pairs * LX, 2 * D), BF16),
            pltpu.VMEM((D, pairs * LX), BF16),
            pltpu.VMEM((pairs, LP, D), BF16),
            pltpu.VMEM((D, D), F32),
            pltpu.VMEM((D, 2 * D), F32),
            pltpu.VMEM(dq.shape, F32),
            pltpu.VMEM((2, 3 * D // 2, D), F32),
            pltpu.SemaphoreType.DMA((pairs,)),
            pltpu.SemaphoreType.DMA(()),
            pltpu.SemaphoreType.DMA((6,)),
        ],
        compiler_params=pltpu.CompilerParams(vmem_limit_bytes=LIMIT),
    )(picks, tangent, core, text, qx, kv_weight, head, dq, gathered, grad)


def ring_scatter(blocks, axis):
    n = lax.axis_size(axis)
    me = lax.axis_index(axis)
    sent = []
    for step in range(1, n):
        piece = lax.dynamic_index_in_dim(blocks, (me + step) % n, 0, keepdims=False)
        sent.append(lax.ppermute(piece, axis, [(k, (k + step) % n) for k in range(n)]))
    return sent, lax.dynamic_index_in_dim(blocks, me, 0, keepdims=False)


def reduce_gradients(mine, other):
    from_core = lax.ppermute(other, "dev_2", [(0, 1), (1, 0)])
    half = mine.shape[0] // 3
    parts = [
        mine[k * half : (k + 1) * half] + from_core[k * half : (k + 1) * half] for k in range(3)
    ]
    for stage in range(3):
        moved = []
        for color in range(3):
            axis = RINGS[ORDERS[color][stage]]
            n = lax.axis_size(axis)
            part = parts[color]
            moved.append(ring_scatter(part.reshape(n, part.shape[0] // n, part.shape[1]), axis))
        parts = []
        for sent, kept in moved:
            for piece in sent:
                kept = kept + piece
            parts.append(kept)
    return parts


def local(image_tokens, text_tokens, negatives, query_weight, kv_weight, match_head, cotangent):
    pairs, text_len, model = text_tokens.shape
    images = jnp.pad(image_tokens, ((0, 0), (0, LP - LI), (0, 0)))
    gathered = lax.all_gather(images, DEV, axis=0, tiled=True)
    text = jnp.pad(text_tokens, ((0, 0), (0, QP - LT), (0, 0))).reshape(pairs * QP, model)
    scale = cotangent.astype(F32) / text_len
    head = match_head.reshape(1, model)
    qx, grad, dq, own_rows = own_pairs(scale[:, 0], text, query_weight, images, kv_weight, head)
    core = lax.axis_index("dev_2").astype(jnp.int32).reshape(1)
    rings = tuple(lax.axis_size(ring) for ring in RINGS)
    mine, other, far_rows = negative_pairs(
        negatives.reshape(-1), scale[:, 1:].reshape(-1), core, text, qx, kv_weight, head, dq, gathered, grad, rings
    )
    own_logits = jnp.sum(own_rows, axis=1, keepdims=True)
    far_logits = jnp.sum(far_rows, axis=1).reshape(pairs, 2)
    logits = jnp.concatenate([own_logits, far_logits], axis=1) / text_len
    grad_query, grad_key, grad_value = reduce_gradients(mine, other)
    return logits, grad_query, jnp.concatenate([grad_key, grad_value], axis=1)


def solution(mesh):
    torus = Mesh(
        mesh.devices.reshape(mesh.shape["grp"], 4, 4, 2), ("grp", "dev_0", "dev_1", "dev_2")
    )
    placed = (
        P(GRP_DEV, None, None),
        P(GRP_DEV, None, None),
        P(GRP_DEV, None),
        P(),
        P(),
        P(),
        P(GRP_DEV, None),
    )
    return jax.shard_map(
        local,
        mesh=torus,
        in_specs=placed,
        out_specs=(P(GRP_DEV, None), P(GRP_DEV, None), P(GRP_DEV, None)),
        check_vma=False,
    )
```

```python
import functools

import jax
import jax.numpy as jnp
from jax import lax
from jax.experimental import pallas as pl
from jax.experimental.pallas import tpu as pltpu
from jax.sharding import Mesh
from jax.sharding import PartitionSpec as P

DEV = ("dev_0", "dev_1", "dev_2")
GRP_DEV = ("grp", "dev_0", "dev_1", "dev_2")
RINGS = ("grp", "dev_0", "dev_1")
ORDERS = ((0, 1, 2), (1, 2, 0), (2, 0, 1))

D = 768
HEADS = 12
LI = 197
LP = 200
LX = 256
LT = 30
QP = 32
GROUPS = 3
GW = 256
ROWS = 128
F32 = jnp.float32
BF16 = jnp.bfloat16


def nn(a, b):
    return lax.dot_general(a, b, (((1,), (0,)), ((), ())), preferred_element_type=F32)


def nt(a, b):
    return lax.dot_general(a, b, (((1,), (1,)), ((), ())), preferred_element_type=F32)


def tn(a, b):
    return lax.dot_general(a, b, (((0,), (0,)), ((), ())), preferred_element_type=F32)


def block_mask():
    row = lax.broadcasted_iota(jnp.int32, (ROWS, GW), 0)
    col = lax.broadcasted_iota(jnp.int32, (ROWS, GW), 1)
    return row, (row // QP) == (col // 64)


def fill_constants(head_ref, mhx_ref, ones_ref):
    row, same = block_mask()
    ones_ref[...] = jnp.where(same & (row % QP < LT), 1.0, 0.0).astype(BF16)
    for g in range(GROUPS):
        rest = head_ref[:, g * GW : (g + 1) * GW]
        for piece in range(3):
            part = rest.astype(BF16)
            rest = rest - part.astype(F32)
            wide = jnp.broadcast_to(part.astype(F32), (ROWS, GW))
            mhx_ref[piece * GROUPS + g] = jnp.where(same, wide, 0.0).astype(BF16)


def attend_pair(i, row, text, scale, keyval, qx_ref, head_ref, mhx_ref, ones_ref, dkv_ref, dq_ref, lrow_ref):
    tail = lax.broadcasted_iota(jnp.int32, (8, ROWS), 0) < (LI - (LP - 8))
    base = pl.multiple_of(i * LX, LX)
    trow = pl.multiple_of(text * QP, QP)
    total = jnp.zeros((1, GW), F32)
    for g in range(GROUPS):
        lo = g * GW
        keys = keyval(lo)
        values = keyval(D + lo)
        query = qx_ref[text * GROUPS + g]
        head = head_ref[:, lo : lo + GW]
        scores = nt(keys, query)
        scores = jnp.concatenate(
            [scores[: LP - 8], jnp.where(tail, scores[LP - 8 :], -1e30)], axis=0
        )
        top = jnp.max(scores, axis=0, keepdims=True)
        expd = jnp.exp(scores - top)
        probs = expd * (1.0 / jnp.sum(expd, axis=0, keepdims=True))
        probs_low = probs.astype(BF16)
        dp = nt(values, mhx_ref[g]) + nt(values, mhx_ref[GROUPS + g]) + nt(values, mhx_ref[2 * GROUPS + g])
        dp = dp * scale
        mean = jnp.sum(probs * dp, axis=0, keepdims=True)
        d_low = (probs * (dp - mean)).astype(BF16)
        dkv_ref[pl.ds(base, LP), lo : lo + GW] = nn(d_low, query).astype(BF16)
        weight = nn(probs_low, ones_ref[...])
        dkv_ref[pl.ds(base, LP), D + lo : D + lo + GW] = (weight * (head * scale)).astype(BF16)
        total = total + jnp.sum(weight * values.astype(F32), axis=0, keepdims=True) * head
        wide = tn(d_low, keys)
        col = lax.broadcasted_iota(jnp.int32, (QP, GW), 1) // 64
        dq = jnp.where(col == 0, wide[:QP], 0.0)
        for h in range(1, 4):
            dq = jnp.where(col == h, wide[h * QP : (h + 1) * QP], dq)
        dq_ref[pl.ds(trow, QP), lo : lo + GW] += dq * 0.125
    lrow_ref[pl.ds(row, 1), :] = total


def own_kernel(
    tan_ref, text_ref, qw_ref, image_ref, kvw_ref, head_ref,
    qx_ref, grad_ref, dq_ref, lrow_ref,
    mhx_ref, ones_ref, kv_ref, dkv_ref, xt_ref,
    *, pairs,
):
    fill_constants(head_ref, mhx_ref, ones_ref)
    dq_ref[...] = jnp.zeros_like(dq_ref)
    dkv_ref[...] = jnp.zeros_like(dkv_ref)
    queries = (nn(text_ref[...], qw_ref[...]).astype(BF16).astype(F32) * 0.125)
    _, same = block_mask()
    for t in range(pairs):
        for g in range(GROUPS):
            part = queries[t * QP : (t + 1) * QP, g * GW : (g + 1) * GW]
            wide = jnp.concatenate([part] * 4, axis=0)
            qx_ref[t * GROUPS + g] = jnp.where(same, wide, 0.0).astype(BF16)

    def one(i, carry):
        image = image_ref[i]
        kv_ref[...] = nn(image, kvw_ref[...]).astype(BF16)
        wide = jnp.concatenate([image, jnp.zeros((LX - LP, D), BF16)], axis=0)
        xt_ref[:, pl.ds(pl.multiple_of(i * LX, LX), LX)] = wide.T
        attend_pair(
            i, i, i, tan_ref[i], lambda lo: kv_ref[:, lo : lo + GW],
            qx_ref, head_ref, mhx_ref, ones_ref, dkv_ref, dq_ref, lrow_ref,
        )
        return carry

    lax.fori_loop(0, pairs, one, 0)

    def block(n, carry):
        cols = pl.ds(pl.multiple_of(n * GW, GW), GW)
        grad_ref[:, cols] = nn(xt_ref[...], dkv_ref[:, cols])
        return carry

    lax.fori_loop(0, 2 * D // GW, block, 0)


def strip_rows(color, rings):
    strips = []
    size = D // (rings[0] * rings[1] * rings[2] * 2)
    for a in range(rings[0]):
        for b in range(rings[1]):
            for c in range(rings[2]):
                at = (a, b, c)
                order = ORDERS[color]
                place = 0
                for ring in order:
                    place = place * rings[ring] + at[ring]
                for core in range(2):
                    source = (((a * rings[1] + b) * rings[2] + c) * 2 + core) * size
                    strips.append((core, source, place * size))
    return size, strips


def locate(negative, spot, rings):
    per_device = 4
    owner = negative // per_device
    inner = negative % per_device
    y_size = rings[2]
    z_off = (owner // (2 * y_size) - spot[0] + rings[1]) % rings[1]
    y_off = ((owner // 2) % y_size - spot[1] + y_size) % y_size
    color = inner // 2
    near = jnp.where(color == 0, y_off, z_off)
    far = jnp.where(color == 0, z_off, y_off)
    half = jnp.where((near == 0) | (near == 3), 0, 1)
    row = inner % 2 + jnp.where((near == 2) | (near == 3), 2, 0)
    kind = jnp.where(far == 0, 0, jnp.where(far == 3, 1, jnp.where(far == 1, 2, 3)))
    other = (owner + spot[2]) % 2
    late = (kind == 3) | ((kind == 1) & (half == 1)) | ((kind == 2) & (half == 0))
    return ((other * 2 + color) * 4 + kind) * 2 + half, row, late


def negatives_kernel(
    pick_ref, tan_ref, spot_ref, text_ref, qx_ref, kvw_ref, head_ref, dq_in_ref, lrow_in_ref, grad_in_ref, *rest,
    pairs, rings, blocks, last,
):
    pieces, rest = rest[: len(blocks)], rest[len(blocks) :]
    if last:
        mine_ref, other_ref, lrow_ref = rest[:3]
    else:
        out_grad_ref, out_dq_ref, lrow_ref = rest[:3]
    (
        mhx_ref, ones_ref, kv_ref, dkv_ref, xt_ref, image_ref, grad_ref, prior_ref, dq_ref, out_ref, list_ref,
        sems, prior_sem, out_sems,
    ) = rest[3:]
    spot = [spot_ref[k] for k in range(3)]
    count = jnp.int32(0)
    for j in range(pairs):
        block, row, late = locate(pick_ref[j], spot, rings)
        here = late == last
        list_ref[count] = j
        for k, piece in enumerate(pieces):

            @pl.when(here & (block == blocks[k]))
            def _():
                pltpu.make_async_copy(piece.at[row], image_ref.at[count], sems.at[count]).start()

        count = count + here.astype(jnp.int32)
    prior = pltpu.make_async_copy(grad_in_ref, prior_ref, prior_sem)
    prior.start()
    fill_constants(head_ref, mhx_ref, ones_ref)
    dq_ref[...] = dq_in_ref[...]
    lrow_ref[...] = lrow_in_ref[...]
    dkv_ref[...] = jnp.zeros_like(dkv_ref)
    xt_ref[...] = jnp.zeros_like(xt_ref)

    def one(i, carry):
        pltpu.make_async_copy(pieces[0].at[0], image_ref.at[i], sems.at[i]).wait()
        j = list_ref[i]
        image = image_ref[i]
        kv_ref[...] = nn(image, kvw_ref[...]).astype(BF16)
        wide = jnp.concatenate([image, jnp.zeros((LX - LP, D), BF16)], axis=0)
        xt_ref[i] = wide.T
        attend_pair(
            i, j, j // 2, tan_ref[j], lambda lo: kv_ref[:, lo : lo + GW],
            qx_ref, head_ref, mhx_ref, ones_ref, dkv_ref, dq_ref, lrow_ref,
        )
        return carry

    lax.fori_loop(0, count, one, 0)
    twos = (count + 1) // 2

    def products(part):
        def two(k, carry):
            left = xt_ref[2 * k]
            right = xt_ref[2 * k + 1]
            rows = pl.ds(pl.multiple_of(2 * k * LX, LX), LX)
            more = pl.ds(pl.multiple_of((2 * k + 1) * LX, LX), LX)

            def cols(n, inner):
                at = pl.ds(pl.multiple_of(n * GW, GW), GW)
                wide = pl.ds(pl.multiple_of(part * D + n * GW, GW), GW)
                prior_ref[:, wide] += nn(left, dkv_ref[rows, wide]) + nn(right, dkv_ref[more, wide])
                return inner

            return lax.fori_loop(0, D // GW, cols, carry)

        lax.fori_loop(0, twos, two, 0)

    if not last:
        prior.wait()
        products(0)
        products(1)
        out_grad_ref[...] = prior_ref[...]
        out_dq_ref[...] = dq_ref[...]
        return

    core = spot[2]
    half = D // 2

    def spread(color, source_ref, lo):
        size, strips = strip_rows(color, rings)
        for which, source, target in strips:
            slot = jnp.where(core == which, 0, 1)
            out_ref[slot, color * half + target : color * half + target + size, :] = source_ref[
                source : source + size, lo : lo + D
            ]
        copies = []
        for slot, ref in ((1, other_ref), (0, mine_ref)):
            copy = pltpu.make_async_copy(
                out_ref.at[slot, pl.ds(color * half, half)],
                ref.at[pl.ds(color * half, half)],
                out_sems.at[2 * color + slot],
            )
            copy.start()
            copies.append(copy)
        return copies

    grad_ref[...] = tn(text_ref[...], dq_ref[...].astype(BF16))
    copies = spread(0, grad_ref, 0)
    prior.wait()
    for part in range(2):
        products(part)
        copies += spread(part + 1, prior_ref, part * D)
    for copy in copies:
        copy.wait()


VM = pl.BlockSpec(memory_space=pltpu.VMEM)
SM = pl.BlockSpec(memory_space=pltpu.SMEM)
ANY = pl.BlockSpec(memory_space=pl.ANY)
LIMIT = 60 * 1024 * 1024


def own_pairs(tangent, text, query_weight, images, kv_weight, head):
    pairs = images.shape[0]
    return pl.pallas_call(
        functools.partial(own_kernel, pairs=pairs),
        name="own_pairs",
        in_specs=[SM] + [VM] * 5,
        out_specs=[VM] * 4,
        out_shape=[
            jax.ShapeDtypeStruct((pairs * GROUPS, ROWS, GW), BF16),
            jax.ShapeDtypeStruct((D, 2 * D), F32),
            jax.ShapeDtypeStruct((pairs * QP, D), F32),
            jax.ShapeDtypeStruct((pairs, GW), F32),
        ],
        scratch_shapes=[
            pltpu.VMEM((3 * GROUPS, ROWS, GW), BF16),
            pltpu.VMEM((ROWS, GW), BF16),
            pltpu.VMEM((LP, 2 * D), BF16),
            pltpu.VMEM((pairs * LX, 2 * D), BF16),
            pltpu.VMEM((D, pairs * LX), BF16),
        ],
        compiler_params=pltpu.CompilerParams(vmem_limit_bytes=LIMIT),
    )(tangent, text, query_weight, images, kv_weight, head)


def negative_pairs(picks, tangent, spot, text, qx, kv_weight, head, dq, lrow, grad, arrived, rings, last):
    pairs = picks.shape[0]
    blocks = tuple(arrived)
    half = jax.ShapeDtypeStruct((3 * D // 2, D), F32)
    rows = jax.ShapeDtypeStruct(lrow.shape, F32)
    if last:
        out_shape, out_specs = [half, half, rows], [ANY, ANY, VM]
    else:
        out_shape = [jax.ShapeDtypeStruct(grad.shape, F32), jax.ShapeDtypeStruct(dq.shape, F32), rows]
        out_specs = [VM] * 3
    return pl.pallas_call(
        functools.partial(negatives_kernel, pairs=pairs, rings=rings, blocks=blocks, last=last),
        name="late_pairs" if last else "early_pairs",
        in_specs=[SM] * 3 + [VM] * 6 + [ANY] * (1 + len(blocks)),
        out_specs=out_specs,
        out_shape=out_shape,
        scratch_shapes=[
            pltpu.VMEM((3 * GROUPS, ROWS, GW), BF16),
            pltpu.VMEM((ROWS, GW), BF16),
            pltpu.VMEM((LP, 2 * D), BF16),
            pltpu.VMEM((pairs * LX, 2 * D), BF16),
            pltpu.VMEM((pairs, D, LX), BF16),
            pltpu.VMEM((pairs, LP, D), BF16),
            pltpu.VMEM((D, D) if last else (8, 128), F32),
            pltpu.VMEM((D, 2 * D), F32),
            pltpu.VMEM(dq.shape, F32),
            pltpu.VMEM((2, 3 * D // 2, D) if last else (2, 8, 128), F32),
            pltpu.SMEM((pairs + 1,), jnp.int32),
            pltpu.SemaphoreType.DMA((pairs + 1,)),
            pltpu.SemaphoreType.DMA(()),
            pltpu.SemaphoreType.DMA((6,)),
        ],
        compiler_params=pltpu.CompilerParams(vmem_limit_bytes=LIMIT),
    )(picks, tangent, spot, text, qx, kv_weight, head, dq, lrow, grad, *arrived.values())


def shift(x, axis, step):
    n = lax.axis_size(axis)
    return lax.ppermute(x, axis, [(k, (k + step) % n) for k in range(n)])


AXES = (("dev_1", "dev_0"), ("dev_0", "dev_1"))


def first_steps(images):
    sent = []
    for color, (near, _) in enumerate(AXES):
        own = images[2 * color : 2 * color + 2]
        sent.append((own, shift(own, near, 1), shift(own, near, -1)))
    return sent


def next_steps(sent):
    arrived = {}
    for color, (near, far) in enumerate(AXES):
        own, left, right = sent[color]
        left_far, right_far = shift(left[:1], near, 1), shift(right[1:], near, -1)
        a = jnp.concatenate([own, left])
        b = jnp.concatenate([right, left_far, right_far])
        left_a, right_b = shift(a, far, 1), shift(b, far, -1)
        left_b, right_a = shift(b, far, 1), shift(a, far, -1)
        for k, block in enumerate((a, b, left_a, left_b, right_a, right_b)):
            arrived[color * 8 + k] = block
            arrived[16 + color * 8 + k] = shift(block, "dev_2", 1)
    return arrived


def last_steps(arrived):
    far_blocks = {}
    for color, (_, far) in enumerate(AXES):
        far_blocks[color * 8 + 6] = shift(arrived[color * 8 + 2], far, 1)
        far_blocks[color * 8 + 7] = shift(arrived[color * 8 + 5], far, -1)
    return far_blocks


def together(blocks, other):
    keys = sorted(blocks)
    out = lax.optimization_barrier((other, *[blocks[k] for k in keys]))
    return dict(zip(keys, out[1:])), out[0]


EARLY = (0, 1, 2, 5)


def ring_scatter(blocks, axis):
    n = lax.axis_size(axis)
    me = lax.axis_index(axis)
    sent = []
    for step in range(1, n):
        piece = lax.dynamic_index_in_dim(blocks, (me + step) % n, 0, keepdims=False)
        sent.append(lax.ppermute(piece, axis, [(k, (k + step) % n) for k in range(n)]))
    return sent, lax.dynamic_index_in_dim(blocks, me, 0, keepdims=False)


def reduce_gradients(mine, other):
    from_core = lax.ppermute(other, "dev_2", [(0, 1), (1, 0)])
    half = mine.shape[0] // 3
    parts = [
        mine[k * half : (k + 1) * half] + from_core[k * half : (k + 1) * half] for k in range(3)
    ]
    for stage in range(3):
        moved = []
        for color in range(3):
            axis = RINGS[ORDERS[color][stage]]
            n = lax.axis_size(axis)
            part = parts[color]
            moved.append(ring_scatter(part.reshape(n, part.shape[0] // n, part.shape[1]), axis))
        parts = []
        for sent, kept in moved:
            for piece in sent:
                kept = kept + piece
            parts.append(kept)
    return parts


def local(image_tokens, text_tokens, negatives, query_weight, kv_weight, match_head, cotangent):
    pairs, text_len, model = text_tokens.shape
    images = jnp.pad(image_tokens, ((0, 0), (0, LP - LI), (0, 0)))
    sent = first_steps(images)
    text = jnp.pad(text_tokens, ((0, 0), (0, QP - LT), (0, 0))).reshape(pairs * QP, model)
    scale = cotangent.astype(F32) / text_len
    head = match_head.reshape(1, model)
    qx, grad, dq, own_rows = own_pairs(scale[:, 0], text, query_weight, images, kv_weight, head)
    arrived = next_steps(sent)
    passed, dq = together({k: v for k, v in arrived.items() if k in (2, 5, 10, 13)}, dq)
    arrived |= passed
    far_blocks = last_steps(arrived)
    spot = jnp.stack([lax.axis_index(axis) for axis in DEV]).astype(jnp.int32)
    rings = tuple(lax.axis_size(ring) for ring in RINGS)
    picks = negatives.reshape(-1)
    far_scale = scale[:, 1:].reshape(-1)
    rows = jnp.zeros((picks.shape[0], GW), F32)
    early = {k: v for k, v in arrived.items() if k % 8 in EARLY}
    grad, dq, rows = negative_pairs(
        picks, far_scale, spot, text, qx, kv_weight, head, dq, rows, grad, early, rings, False
    )
    far_blocks, dq = together(far_blocks, dq)
    late = {k: v for k, v in arrived.items() if k % 8 not in EARLY}
    late |= far_blocks | {16 + k: shift(v, "dev_2", 1) for k, v in far_blocks.items()}
    mine, other, rows = negative_pairs(
        picks, far_scale, spot, text, qx, kv_weight, head, dq, rows, grad, late, rings, True
    )
    own_logits = jnp.sum(own_rows, axis=1, keepdims=True)
    far_logits = jnp.sum(rows, axis=1).reshape(pairs, 2)
    logits = jnp.concatenate([own_logits, far_logits], axis=1) / text_len
    grad_query, grad_key, grad_value = reduce_gradients(mine, other)
    return logits, grad_query, jnp.concatenate([grad_key, grad_value], axis=1)


def solution(mesh):
    torus = Mesh(
        mesh.devices.reshape(mesh.shape["grp"], 4, 4, 2), ("grp", "dev_0", "dev_1", "dev_2")
    )
    placed = (
        P(GRP_DEV, None, None),
        P(GRP_DEV, None, None),
        P(GRP_DEV, None),
        P(),
        P(),
        P(),
        P(GRP_DEV, None),
    )
    return jax.shard_map(
        local,
        mesh=torus,
        in_specs=placed,
        out_specs=(P(GRP_DEV, None), P(GRP_DEV, None), P(GRP_DEV, None)),
        check_vma=False,
    )
```

```python
import functools

import jax
import jax.numpy as jnp
from jax import lax
from jax.experimental import pallas as pl
from jax.experimental.pallas import tpu as pltpu
from jax.sharding import Mesh
from jax.sharding import PartitionSpec as P


DEV = ("dev_0", "dev_1", "dev_2")
GRP_DEV = ("grp", "dev_0", "dev_1", "dev_2")
RINGS = ("grp", "dev_0", "dev_1")
ORDERS = ((0, 2, 1), (1, 2, 0), (2, 1, 0))

D = 768
LI = 197
LP = 200
LX = 256
LT = 30
QP = 32
GROUPS = 3
GW = 256
ROWS = 128
F32 = jnp.float32
BF16 = jnp.bfloat16


def nn(a, b):
    return lax.dot_general(a, b, (((1,), (0,)), ((), ())), preferred_element_type=F32)


def nt(a, b):
    return lax.dot_general(a, b, (((1,), (1,)), ((), ())), preferred_element_type=F32)


def tn(a, b):
    return lax.dot_general(a, b, (((0,), (0,)), ((), ())), preferred_element_type=F32)


def block_mask():
    row = lax.broadcasted_iota(jnp.int32, (ROWS, GW), 0)
    col = lax.broadcasted_iota(jnp.int32, (ROWS, GW), 1)
    return row, (row // QP) == (col // 64)


def fill_constants(head_ref, mhx_ref, ones_ref):
    row, same = block_mask()
    ones_ref[...] = jnp.where(same & (row % QP < LT), 1.0, 0.0).astype(BF16)
    for g in range(GROUPS):
        rest = head_ref[:, g * GW : (g + 1) * GW]
        for piece in range(3):
            part = rest.astype(BF16)
            rest = rest - part.astype(F32)
            wide = jnp.broadcast_to(part.astype(F32), (ROWS, GW))
            mhx_ref[piece * GROUPS + g] = jnp.where(same, wide, 0.0).astype(BF16)


def attend_pair(i, row, text, scale, keyval, qx_ref, head_ref, mhx_ref, ones_ref, dkv_ref, dq_ref, lrow_ref):
    tail = lax.broadcasted_iota(jnp.int32, (8, ROWS), 0) < (LI - (LP - 8))
    base = pl.multiple_of(i * LX, LX)
    trow = pl.multiple_of(text * QP, QP)
    total = jnp.zeros((1, GW), F32)
    for g in range(GROUPS):
        lo = g * GW
        keys = keyval(lo)
        values = keyval(D + lo)
        query = qx_ref[text * GROUPS + g]
        head = head_ref[:, lo : lo + GW]
        scores = nt(keys, query)
        scores = jnp.concatenate(
            [scores[: LP - 8], jnp.where(tail, scores[LP - 8 :], -1e30)], axis=0
        )
        top = jnp.max(scores, axis=0, keepdims=True)
        expd = jnp.exp(scores - top)
        probs = expd * (1.0 / jnp.sum(expd, axis=0, keepdims=True))
        probs_low = probs.astype(BF16)
        dp = nt(values, mhx_ref[g]) + nt(values, mhx_ref[GROUPS + g]) + nt(values, mhx_ref[2 * GROUPS + g])
        dp = dp * scale
        mean = jnp.sum(probs * dp, axis=0, keepdims=True)
        d_low = (probs * (dp - mean)).astype(BF16)
        dkv_ref[pl.ds(base, LP), lo : lo + GW] = nn(d_low, query).astype(BF16)
        weight = nn(probs_low, ones_ref[...])
        dkv_ref[pl.ds(base, LP), D + lo : D + lo + GW] = (weight * (head * scale)).astype(BF16)
        total = total + jnp.sum(weight * values.astype(F32), axis=0, keepdims=True) * head
        wide = tn(d_low, keys)
        col = lax.broadcasted_iota(jnp.int32, (QP, GW), 1) // 64
        dq = jnp.where(col == 0, wide[:QP], 0.0)
        for h in range(1, 4):
            dq = jnp.where(col == h, wide[h * QP : (h + 1) * QP], dq)
        dq_ref[pl.ds(trow, QP), lo : lo + GW] += dq * 0.125
    lrow_ref[pl.ds(row, 1), :] = total


def own_kernel(
    tan_ref, text_ref, qw_ref, image_ref, kvw_ref, head_ref,
    qx_ref, mhx_ref, ones_ref, grad_ref, dq_ref, lrow_ref,
    kv_ref, dkv_ref, xt_ref,
    *, pairs,
):
    fill_constants(head_ref, mhx_ref, ones_ref)
    dq_ref[...] = jnp.zeros_like(dq_ref)
    dkv_ref[...] = jnp.zeros_like(dkv_ref)
    queries = (nn(text_ref[...], qw_ref[...]).astype(BF16).astype(F32) * 0.125)
    _, same = block_mask()
    for t in range(pairs):
        for g in range(GROUPS):
            part = queries[t * QP : (t + 1) * QP, g * GW : (g + 1) * GW]
            wide = jnp.concatenate([part] * 4, axis=0)
            qx_ref[t * GROUPS + g] = jnp.where(same, wide, 0.0).astype(BF16)

    def one(i, carry):
        image = image_ref[i]
        kv_ref[...] = nn(image, kvw_ref[...]).astype(BF16)
        wide = jnp.concatenate([image, jnp.zeros((LX - LP, D), BF16)], axis=0)
        xt_ref[:, pl.ds(pl.multiple_of(i * LX, LX), LX)] = wide.T
        attend_pair(
            i, i, i, tan_ref[i], lambda lo: kv_ref[:, lo : lo + GW],
            qx_ref, head_ref, mhx_ref, ones_ref, dkv_ref, dq_ref, lrow_ref,
        )
        return carry

    lax.fori_loop(0, pairs, one, 0)

    def block(n, carry):
        cols = pl.ds(pl.multiple_of(n * GW, GW), GW)
        grad_ref[:, cols] = nn(xt_ref[...], dkv_ref[:, cols])
        return carry

    lax.fori_loop(0, 2 * D // GW, block, 0)


def strip_rows(color, rings):
    strips = []
    size = D // (rings[0] * rings[1] * rings[2] * 2)
    for a in range(rings[0]):
        for b in range(rings[1]):
            for c in range(rings[2]):
                at = (a, b, c)
                order = ORDERS[color]
                place = 0
                for ring in order:
                    place = place * rings[ring] + at[ring]
                for core in range(2):
                    source = (((a * rings[1] + b) * rings[2] + c) * 2 + core) * size
                    strips.append((core, source, place * size))
    return size, strips


def locate(negative, spot, rings):
    per_device = 4
    owner = negative // per_device
    inner = negative % per_device
    y_size = rings[2]
    z_off = (owner // (2 * y_size) - spot[0] + rings[1]) % rings[1]
    y_off = ((owner // 2) % y_size - spot[1] + y_size) % y_size
    color = inner // 2
    near = jnp.where(color == 0, y_off, z_off)
    far = jnp.where(color == 0, z_off, y_off)
    half = jnp.where((near == 0) | (near == 3), 0, 1)
    row = inner % 2 + jnp.where((near == 2) | (near == 3), 2, 0)
    kind = jnp.where(far == 0, 0, jnp.where(far == 3, 1, jnp.where(far == 1, 2, 3)))
    other = (owner + spot[2]) % 2
    number = kind * 2 + half
    phase = jnp.where(kind == 3, 2, jnp.where((number == 3) | (number == 4), 1, 0))
    return (other * 2 + color) * 8 + number, row, phase


def negatives_kernel(
    pick_ref, tan_ref, spot_ref, text_ref, qx_ref, mhx_ref, ones_ref, kvw_ref, head_ref, dq_in_ref, lrow_in_ref,
    grad_in_ref, *rest,
    pairs, rings, blocks, phase,
):
    last = phase == 2
    pieces, rest = rest[: len(blocks)], rest[len(blocks) :]
    if last:
        mine_ref, other_ref, lrow_ref = rest[:3]
    else:
        out_grad_ref, out_dq_ref, lrow_ref = rest[:3]
    (
        kv_ref, dkv_ref, xt_ref, image_ref, grad_ref, prior_ref, dq_ref, out_ref, list_ref,
        sems, prior_sem, out_sems,
    ) = rest[3:]
    spot = [spot_ref[k] for k in range(3)]
    count = jnp.int32(0)
    for j in range(pairs):
        block, row, when = locate(pick_ref[j], spot, rings)
        here = when == phase
        list_ref[count] = j
        for k, piece in enumerate(pieces):

            @pl.when(here & (block == blocks[k]))
            def _():
                pltpu.make_async_copy(piece.at[row], image_ref.at[count], sems.at[count]).start()

        count = count + here.astype(jnp.int32)
    prior = pltpu.make_async_copy(grad_in_ref, prior_ref, prior_sem)
    prior.start()
    dq_ref[...] = dq_in_ref[...]
    lrow_ref[...] = lrow_in_ref[...]

    def one(i, carry):
        dkv_ref[pl.ds(pl.multiple_of(i * LX + LP - 8, 64), LX - LP + 8), :] = jnp.zeros((LX - LP + 8, 2 * D), BF16)
        pltpu.make_async_copy(pieces[0].at[0], image_ref.at[i], sems.at[i]).wait()
        j = list_ref[i]
        image = image_ref[i]
        kv_ref[...] = nn(image, kvw_ref[...]).astype(BF16)
        wide = jnp.concatenate([image, jnp.zeros((LX - LP, D), BF16)], axis=0)
        xt_ref[i] = wide.T
        attend_pair(
            i, j, j // 2, tan_ref[j], lambda lo: kv_ref[:, lo : lo + GW],
            qx_ref, head_ref, mhx_ref, ones_ref, dkv_ref, dq_ref, lrow_ref,
        )
        return carry

    lax.fori_loop(0, count, one, 0)
    twos = (count + 1) // 2

    @pl.when(count % 2 == 1)
    def _():
        dkv_ref[pl.ds(pl.multiple_of(count * LX, LX), LX), :] = jnp.zeros((LX, 2 * D), BF16)
        xt_ref[count] = jnp.zeros((D, LX), BF16)

    def products(part):
        def two(k, carry):
            left = xt_ref[2 * k]
            right = xt_ref[2 * k + 1]
            rows = pl.ds(pl.multiple_of(2 * k * LX, LX), LX)
            more = pl.ds(pl.multiple_of((2 * k + 1) * LX, LX), LX)

            def cols(n, inner):
                at = pl.ds(pl.multiple_of(n * GW, GW), GW)
                wide = pl.ds(pl.multiple_of(part * D + n * GW, GW), GW)
                prior_ref[:, wide] += nn(left, dkv_ref[rows, wide]) + nn(right, dkv_ref[more, wide])
                return inner

            return lax.fori_loop(0, D // GW, cols, carry)

        lax.fori_loop(0, twos, two, 0)

    if not last:
        prior.wait()
        products(0)
        products(1)
        out_grad_ref[...] = prior_ref[...]
        out_dq_ref[...] = dq_ref[...]
        return

    core = spot[2]
    half = D // 2

    def spread(color, source_ref, lo):
        size, strips = strip_rows(color, rings)
        for which, source, target in strips:
            slot = jnp.where(core == which, 0, 1)
            out_ref[slot, color * half + target : color * half + target + size, :] = source_ref[
                source : source + size, lo : lo + D
            ]
        copies = []
        for slot, ref in ((1, other_ref), (0, mine_ref)):
            copy = pltpu.make_async_copy(
                out_ref.at[slot, pl.ds(color * half, half)],
                ref.at[pl.ds(color * half, half)],
                out_sems.at[2 * color + slot],
            )
            copy.start()
            copies.append(copy)
        return copies

    grad_ref[...] = tn(text_ref[...], dq_ref[...].astype(BF16))
    copies = spread(0, grad_ref, 0)
    prior.wait()
    for part in range(2):
        products(part)
        copies += spread(part + 1, prior_ref, part * D)
    for copy in copies:
        copy.wait()


VM = pl.BlockSpec(memory_space=pltpu.VMEM)
SM = pl.BlockSpec(memory_space=pltpu.SMEM)
ANY = pl.BlockSpec(memory_space=pl.ANY)
LIMIT = 60 * 1024 * 1024


def own_pairs(tangent, text, query_weight, images, kv_weight, head):
    pairs = images.shape[0]
    return pl.pallas_call(
        functools.partial(own_kernel, pairs=pairs),
        name="own_pairs",
        in_specs=[SM] + [VM] * 5,
        out_specs=[VM] * 6,
        out_shape=[
            jax.ShapeDtypeStruct((pairs * GROUPS, ROWS, GW), BF16),
            jax.ShapeDtypeStruct((3 * GROUPS, ROWS, GW), BF16),
            jax.ShapeDtypeStruct((ROWS, GW), BF16),
            jax.ShapeDtypeStruct((D, 2 * D), F32),
            jax.ShapeDtypeStruct((pairs * QP, D), F32),
            jax.ShapeDtypeStruct((pairs, GW), F32),
        ],
        scratch_shapes=[
            pltpu.VMEM((LP, 2 * D), BF16),
            pltpu.VMEM((pairs * LX, 2 * D), BF16),
            pltpu.VMEM((D, pairs * LX), BF16),
        ],
        compiler_params=pltpu.CompilerParams(vmem_limit_bytes=LIMIT),
    )(tangent, text, query_weight, images, kv_weight, head)


def negative_pairs(picks, tangent, spot, text, made, kv_weight, head, dq, lrow, grad, arrived, rings, phase):
    last = phase == 2
    pairs = picks.shape[0]
    blocks = tuple(arrived)
    half = jax.ShapeDtypeStruct((3 * D // 2, D), F32)
    rows = jax.ShapeDtypeStruct(lrow.shape, F32)
    if last:
        out_shape, out_specs = [half, half, rows], [ANY, ANY, VM]
    else:
        out_shape = [jax.ShapeDtypeStruct(grad.shape, F32), jax.ShapeDtypeStruct(dq.shape, F32), rows]
        out_specs = [VM] * 3
    return pl.pallas_call(
        functools.partial(negatives_kernel, pairs=pairs, rings=rings, blocks=blocks, phase=phase),
        in_specs=[SM] * 3 + [VM] * 8 + [ANY] * (1 + len(blocks)),
        out_specs=out_specs,
        out_shape=out_shape,
        scratch_shapes=[
            pltpu.VMEM((LP, 2 * D), BF16),
            pltpu.VMEM((pairs * LX, 2 * D), BF16),
            pltpu.VMEM((pairs, D, LX), BF16),
            pltpu.VMEM((pairs, LP, D), BF16),
            pltpu.VMEM((D, D) if last else (8, 128), F32),
            pltpu.VMEM((D, 2 * D), F32),
            pltpu.VMEM(dq.shape, F32),
            pltpu.VMEM((2, 3 * D // 2, D) if last else (2, 8, 128), F32),
            pltpu.SMEM((pairs + 1,), jnp.int32),
            pltpu.SemaphoreType.DMA((pairs + 1,)),
            pltpu.SemaphoreType.DMA(()),
            pltpu.SemaphoreType.DMA((6,)),
        ],
        compiler_params=pltpu.CompilerParams(vmem_limit_bytes=LIMIT),
    )(picks, tangent, spot, text, *made, kv_weight, head, dq, lrow, grad, *arrived.values())


def shift(x, axis, step):
    n = lax.axis_size(axis)
    return lax.ppermute(x, axis, [(k, (k + step) % n) for k in range(n)])


AXES = (("dev_1", "dev_0"), ("dev_0", "dev_1"))


def first_steps(images):
    blocks = []
    for color, (near, _) in enumerate(AXES):
        own = images[2 * color : 2 * color + 2]
        blocks.append((own, shift(own, near, 1), shift(own, near, -1)))
    return blocks


def other_core(blocks):
    return blocks | {16 + k: shift(block, "dev_2", 1) for k, block in blocks.items()}


def next_steps(first):
    soon, then = {}, {}
    for color, (near, far) in enumerate(AXES):
        own, left, right = first[color]
        left_far, right_far = shift(left[:1], near, 1), shift(right[1:], near, -1)
        a = jnp.concatenate([own, left])
        b = jnp.concatenate([right, left_far, right_far])
        soon[color * 8] = a
        soon[color * 8 + 1] = b
        soon[color * 8 + 2] = shift(a, far, 1)
        soon[color * 8 + 5] = shift(b, far, -1)
        then[color * 8 + 3] = shift(b, far, 1)
        then[color * 8 + 4] = shift(a, far, -1)
    return soon, then


def last_steps(soon):
    blocks = {}
    for color, (_, far) in enumerate(AXES):
        blocks[color * 8 + 6] = shift(soon[color * 8 + 2], far, 1)
        blocks[color * 8 + 7] = shift(soon[color * 8 + 5], far, -1)
    return blocks


def together(blocks, other):
    keys = sorted(blocks)
    out = lax.optimization_barrier((other, *[blocks[k] for k in keys]))
    return dict(zip(keys, out[1:])), out[0]


def ring_scatter(blocks, axis):
    n = lax.axis_size(axis)
    me = lax.axis_index(axis)
    sent = []
    for step in range(1, n):
        piece = lax.dynamic_index_in_dim(blocks, (me + step) % n, 0, keepdims=False)
        sent.append(lax.ppermute(piece, axis, [(k, (k + step) % n) for k in range(n)]))
    return sent, lax.dynamic_index_in_dim(blocks, me, 0, keepdims=False)


def reduce_gradients(mine, other):
    from_core = lax.ppermute(other, "dev_2", [(0, 1), (1, 0)])
    half = mine.shape[0] // 3
    parts = [
        mine[k * half : (k + 1) * half] + from_core[k * half : (k + 1) * half] for k in range(3)
    ]
    width = mine.shape[1]
    for stage in range(3):
        moved = []
        for ring, axis in enumerate(RINGS):
            colors = [k for k in range(3) if ORDERS[k][stage] == ring]
            if not colors:
                continue
            n = lax.axis_size(axis)
            blocks = [parts[k].reshape(n, parts[k].shape[0] // n, width) for k in colors]
            rows = blocks[0].shape[1]
            moved.append((colors, rows, ring_scatter(jnp.concatenate(blocks, axis=1), axis)))
        for colors, rows, (sent, kept) in moved:
            for piece in sent:
                kept = kept + piece
            for place, k in enumerate(colors):
                parts[k] = kept[place * rows : (place + 1) * rows]
    return parts


def local(image_tokens, text_tokens, negatives, query_weight, kv_weight, match_head, cotangent):
    pairs, text_len, model = text_tokens.shape
    images = jnp.pad(image_tokens, ((0, 0), (0, LP - LI), (0, 0)))
    first = first_steps(images)
    text = jnp.pad(text_tokens, ((0, 0), (0, QP - LT), (0, 0))).reshape(pairs * QP, model)
    scale = cotangent.astype(F32) / text_len
    head = match_head.reshape(1, model)
    *made, grad, dq, own_rows = own_pairs(scale[:, 0], text, query_weight, images, kv_weight, head)
    soon, then = next_steps(first)
    passed, dq = together({k: v for k, v in soon.items() if k % 8 in (2, 5)}, dq)
    soon |= passed
    far_blocks = last_steps(soon)
    spot = jnp.stack([lax.axis_index(axis) for axis in DEV]).astype(jnp.int32)
    rings = tuple(lax.axis_size(ring) for ring in RINGS)
    picks = negatives.reshape(-1)
    far_scale = scale[:, 1:].reshape(-1)
    rows = jnp.zeros((picks.shape[0], GW), F32)
    grad, dq, rows = negative_pairs(
        picks, far_scale, spot, text, made, kv_weight, head, dq, rows, grad, other_core(soon), rings, 0
    )
    then, dq = together(then, dq)
    grad, dq, rows = negative_pairs(
        picks, far_scale, spot, text, made, kv_weight, head, dq, rows, grad, other_core(then), rings, 1
    )
    far_blocks, dq = together(far_blocks, dq)
    mine, other, rows = negative_pairs(
        picks, far_scale, spot, text, made, kv_weight, head, dq, rows, grad, other_core(far_blocks), rings, 2
    )
    own_logits = jnp.sum(own_rows, axis=1, keepdims=True)
    far_logits = jnp.sum(rows, axis=1).reshape(pairs, 2)
    logits = jnp.concatenate([own_logits, far_logits], axis=1) / text_len
    grad_query, grad_key, grad_value = reduce_gradients(mine, other)
    return logits, grad_query, jnp.concatenate([grad_key, grad_value], axis=1)


def solution(mesh):
    torus = Mesh(
        mesh.devices.reshape(mesh.shape["grp"], 4, 4, 2), ("grp", "dev_0", "dev_1", "dev_2")
    )
    placed = (
        P(GRP_DEV, None, None),
        P(GRP_DEV, None, None),
        P(GRP_DEV, None),
        P(),
        P(),
        P(),
        P(GRP_DEV, None),
    )
    return jax.shard_map(
        local,
        mesh=torus,
        in_specs=placed,
        out_specs=(P(GRP_DEV, None), P(GRP_DEV, None), P(GRP_DEV, None)),
        check_vma=False,
    )
```

```python
import functools

import jax
import jax.numpy as jnp
from jax import lax
from jax.experimental import pallas as pl
from jax.experimental.pallas import tpu as pltpu
from jax.sharding import Mesh
from jax.sharding import PartitionSpec as P


DEV = ("dev_0", "dev_1", "dev_2")
GRP_DEV = ("grp", "dev_0", "dev_1", "dev_2")
RINGS = ("grp", "dev_0", "dev_1")
ORDERS = ((0, 2, 1), (1, 2, 0), (2, 1, 0))

D = 768
LI = 197
LP = 200
LX = 256
LT = 30
QP = 32
GROUPS = 3
GW = 256
ROWS = 128
F32 = jnp.float32
BF16 = jnp.bfloat16


def nn(a, b):
    return lax.dot_general(a, b, (((1,), (0,)), ((), ())), preferred_element_type=F32)


def nt(a, b):
    return lax.dot_general(a, b, (((1,), (1,)), ((), ())), preferred_element_type=F32)


def tn(a, b):
    return lax.dot_general(a, b, (((0,), (0,)), ((), ())), preferred_element_type=F32)


def block_mask():
    row = lax.broadcasted_iota(jnp.int32, (ROWS, GW), 0)
    col = lax.broadcasted_iota(jnp.int32, (ROWS, GW), 1)
    return row, (row // QP) == (col // 64)


def fill_constants(head_ref, mhx_ref, ones_ref):
    row, same = block_mask()
    ones_ref[...] = jnp.where(same & (row % QP < LT), 1.0, 0.0).astype(BF16)
    for g in range(GROUPS):
        rest = head_ref[:, g * GW : (g + 1) * GW]
        for piece in range(3):
            part = rest.astype(BF16)
            rest = rest - part.astype(F32)
            wide = jnp.broadcast_to(part.astype(F32), (ROWS, GW))
            mhx_ref[piece * GROUPS + g] = jnp.where(same, wide, 0.0).astype(BF16)


def attend_pair(i, row, text, scale, keyval, qx_ref, head_ref, mhx_ref, ones_ref, dkv_ref, dq_ref, lrow_ref):
    tail = lax.broadcasted_iota(jnp.int32, (8, ROWS), 0) < (LI - (LP - 8))
    base = pl.multiple_of(i * LX, LX)
    trow = pl.multiple_of(text * QP, QP)
    total = jnp.zeros((1, GW), F32)
    for g in range(GROUPS):
        lo = g * GW
        keys = keyval(lo)
        values = keyval(D + lo)
        query = qx_ref[text * GROUPS + g]
        head = head_ref[:, lo : lo + GW]
        scores = nt(keys, query)
        scores = jnp.concatenate(
            [scores[: LP - 8], jnp.where(tail, scores[LP - 8 :], -1e30)], axis=0
        )
        top = jnp.max(scores, axis=0, keepdims=True)
        expd = jnp.exp(scores - top)
        probs = expd * (1.0 / jnp.sum(expd, axis=0, keepdims=True))
        probs_low = probs.astype(BF16)
        dp = nt(values, mhx_ref[g]) + nt(values, mhx_ref[GROUPS + g]) + nt(values, mhx_ref[2 * GROUPS + g])
        dp = dp * scale
        mean = jnp.sum(probs * dp, axis=0, keepdims=True)
        d_low = (probs * (dp - mean)).astype(BF16)
        dkv_ref[pl.ds(base, LP), lo : lo + GW] = nn(d_low, query).astype(BF16)
        weight = nn(probs_low, ones_ref[...])
        dkv_ref[pl.ds(base, LP), D + lo : D + lo + GW] = (weight * (head * scale)).astype(BF16)
        total = total + jnp.sum(weight * values.astype(F32), axis=0, keepdims=True) * head
        wide = tn(d_low, keys)
        col = lax.broadcasted_iota(jnp.int32, (QP, GW), 1) // 64
        dq = jnp.where(col == 0, wide[:QP], 0.0)
        for h in range(1, 4):
            dq = jnp.where(col == h, wide[h * QP : (h + 1) * QP], dq)
        dq_ref[pl.ds(trow, QP), lo : lo + GW] += dq * 0.125
    lrow_ref[pl.ds(row, 1), :] = total


def own_kernel(
    tan_ref, text_ref, far_text_ref, qw_ref, image_ref, kvw_ref, head_ref,
    qx_ref, mhx_ref, ones_ref, grad_ref, dq_ref, lrow_ref,
    kv_ref, dkv_ref, xt_ref,
    *, pairs,
):
    fill_constants(head_ref, mhx_ref, ones_ref)
    dq_ref[...] = jnp.zeros_like(dq_ref)
    dkv_ref[...] = jnp.zeros_like(dkv_ref)
    _, same = block_mask()
    real = lax.broadcasted_iota(jnp.int32, (pairs * QP, D), 0) % QP < LT
    for side, tokens in enumerate((text_ref, far_text_ref)):
        queries = nn(tokens[...], qw_ref[...]).astype(BF16).astype(F32) * 0.125
        queries = jnp.where(real, queries, 0.0)
        for t in range(pairs):
            for g in range(GROUPS):
                part = queries[t * QP : (t + 1) * QP, g * GW : (g + 1) * GW]
                wide = jnp.concatenate([part] * 4, axis=0)
                qx_ref[(side * pairs + t) * GROUPS + g] = jnp.where(same, wide, 0.0).astype(BF16)

    def one(i, carry):
        image = image_ref[i]
        kv_ref[...] = nn(image, kvw_ref[...]).astype(BF16)
        wide = jnp.concatenate([image, jnp.zeros((LX - LP, D), BF16)], axis=0)
        xt_ref[:, pl.ds(pl.multiple_of(i * LX, LX), LX)] = wide.T
        attend_pair(
            i, i, i, tan_ref[i], lambda lo: kv_ref[:, lo : lo + GW],
            qx_ref, head_ref, mhx_ref, ones_ref, dkv_ref, dq_ref, lrow_ref,
        )
        return carry

    lax.fori_loop(0, pairs, one, 0)

    def block(n, carry):
        cols = pl.ds(pl.multiple_of(n * GW, GW), GW)
        grad_ref[:, cols] = nn(xt_ref[...], dkv_ref[:, cols])
        return carry

    lax.fori_loop(0, 2 * D // GW, block, 0)


def strip_rows(color, rings):
    strips = []
    size = D // (rings[0] * rings[1] * rings[2] * 2)
    for a in range(rings[0]):
        for b in range(rings[1]):
            for c in range(rings[2]):
                at = (a, b, c)
                order = ORDERS[color]
                place = 0
                for ring in order:
                    place = place * rings[ring] + at[ring]
                for core in range(2):
                    source = (((a * rings[1] + b) * rings[2] + c) * 2 + core) * size
                    strips.append((core, source, place * size))
    return size, strips


def locate(negative, spot, rings):
    per_device = 4
    owner = negative // per_device
    inner = negative % per_device
    y_size = rings[2]
    z_off = (owner // (2 * y_size) - spot[0] + rings[1]) % rings[1]
    y_off = ((owner // 2) % y_size - spot[1] + y_size) % y_size
    color = inner // 2
    near = jnp.where(color == 0, y_off, z_off)
    far = jnp.where(color == 0, z_off, y_off)
    half = jnp.where((near == 0) | (near == 3), 0, 1)
    row = inner % 2 + jnp.where((near == 2) | (near == 3), 2, 0)
    kind = jnp.where(far == 0, 0, jnp.where(far == 3, 1, jnp.where(far == 1, 2, 3)))
    number = kind * 2 + half
    phase = jnp.where(kind == 3, 2, jnp.where((number == 3) | (number == 4), 1, 0))
    phase = jnp.where(owner % 2 == spot[2], phase, 3)
    return color * 8 + number, row, phase


def negatives_kernel(
    pick_ref, tan_ref, spot_ref, qx_ref, mhx_ref, ones_ref, kvw_ref, head_ref, dq_in_ref, lrow_in_ref,
    grad_in_ref, *rest,
    pairs, rings, blocks, phase,
):
    last = phase == 2
    pieces, rest = rest[: len(blocks)], rest[len(blocks) :]
    if last:
        mine_ref, other_ref, own_dq_ref, give_ref, lrow_ref = rest[:5]
        rest = rest[5:]
    else:
        out_grad_ref, dq_ref, lrow_ref = rest[:3]
        rest = rest[3:] + (dq_ref,)
    kv_ref, dkv_ref, xt_ref, image_ref, prior_ref, out_ref, list_ref, sems, prior_sem, out_sems, dq_ref = rest
    spot = [spot_ref[k] for k in range(3)]
    count = jnp.int32(0)
    for j in range(pairs):
        block, row, when = locate(pick_ref[j], spot, rings)
        here = when == phase
        list_ref[count] = j
        for k, piece in enumerate(pieces):

            @pl.when(here & (block == blocks[k]))
            def _():
                pltpu.make_async_copy(piece.at[row], image_ref.at[count], sems.at[count]).start()

        count = count + here.astype(jnp.int32)
    prior = pltpu.make_async_copy(grad_in_ref, prior_ref, prior_sem)
    prior.start()
    dq_ref[...] = dq_in_ref[...]
    lrow_ref[...] = lrow_in_ref[...]

    def one(i, carry):
        dkv_ref[pl.ds(pl.multiple_of(i * LX + LP - 8, 64), LX - LP + 8), :] = jnp.zeros((LX - LP + 8, 2 * D), BF16)
        pltpu.make_async_copy(pieces[0].at[0], image_ref.at[i], sems.at[i]).wait()
        j = list_ref[i]
        image = image_ref[i]
        kv_ref[...] = nn(image, kvw_ref[...]).astype(BF16)
        wide = jnp.concatenate([image, jnp.zeros((LX - LP, D), BF16)], axis=0)
        xt_ref[i] = wide.T
        attend_pair(
            i, j, j // 2, tan_ref[j], lambda lo: kv_ref[:, lo : lo + GW],
            qx_ref, head_ref, mhx_ref, ones_ref, dkv_ref, dq_ref, lrow_ref,
        )
        return carry

    lax.fori_loop(0, count, one, 0)
    twos = (count + 1) // 2

    @pl.when(count % 2 == 1)
    def _():
        dkv_ref[pl.ds(pl.multiple_of(count * LX, LX), LX), :] = jnp.zeros((LX, 2 * D), BF16)
        xt_ref[count] = jnp.zeros((D, LX), BF16)

    def products(part):
        def two(k, carry):
            left = xt_ref[2 * k]
            right = xt_ref[2 * k + 1]
            rows = pl.ds(pl.multiple_of(2 * k * LX, LX), LX)
            more = pl.ds(pl.multiple_of((2 * k + 1) * LX, LX), LX)

            def cols(n, inner):
                at = pl.ds(pl.multiple_of(n * GW, GW), GW)
                wide = pl.ds(pl.multiple_of(part * D + n * GW, GW), GW)
                prior_ref[:, wide] += nn(left, dkv_ref[rows, wide]) + nn(right, dkv_ref[more, wide])
                return inner

            return lax.fori_loop(0, D // GW, cols, carry)

        lax.fori_loop(0, twos, two, 0)

    prior.wait()
    if not last:
        copies = []
        for part in range(2):
            products(part)
            cols = pl.ds(part * D, D)
            copies.append(
                pltpu.make_async_copy(prior_ref.at[:, cols], out_grad_ref.at[:, cols], out_sems.at[part])
            )
            copies[-1].start()
    else:
        rows = own_dq_ref.shape[0]
        own_dq_ref[...] = dq_ref[:rows]
        give_ref[:rows] = dq_ref[rows:]
        give_ref[rows:] = jnp.zeros((pairs // 2, D), F32)
        give_ref[rows:, :GW] = lrow_ref[pairs // 2 :]
        copies = []
        for part in range(2):
            products(part)
            copies += spread(part + 1, part, prior_ref, part * D, out_ref, mine_ref, other_ref, out_sems, spot[2], rings)
    for copy in copies:
        copy.wait()


def spread(color, place, source_ref, lo, out_ref, mine_ref, other_ref, sems, core, rings):
    half = D // 2
    size, strips = strip_rows(color, rings)
    for which, source, target in strips:
        slot = jnp.where(core == which, 0, 1)
        out_ref[slot, place * half + target : place * half + target + size, :] = source_ref[
            source : source + size, lo : lo + D
        ]
    copies = []
    for slot, ref in ((1, other_ref), (0, mine_ref)):
        copy = pltpu.make_async_copy(
            out_ref.at[slot, pl.ds(place * half, half)],
            ref.at[pl.ds(place * half, half)],
            sems.at[2 * place + slot],
        )
        copy.start()
        copies.append(copy)
    return copies


def query_kernel(
    spot_ref, text_ref, dq_ref, got_ref, mine_ref, other_ref, grad_ref, out_ref, sems, *, rings
):
    rows = text_ref.shape[0]
    total = dq_ref[:rows] + got_ref[:rows]
    grad_ref[...] = tn(text_ref[...], total.astype(BF16))
    for copy in spread(0, 0, grad_ref, 0, out_ref, mine_ref, other_ref, sems, spot_ref[2], rings):
        copy.wait()


VM = pl.BlockSpec(memory_space=pltpu.VMEM)
SM = pl.BlockSpec(memory_space=pltpu.SMEM)
ANY = pl.BlockSpec(memory_space=pl.ANY)
LIMIT = 60 * 1024 * 1024


def own_pairs(tangent, text, far_text, query_weight, images, kv_weight, head):
    pairs = images.shape[0]
    return pl.pallas_call(
        functools.partial(own_kernel, pairs=pairs),
        name="own_pairs",
        in_specs=[SM] + [VM] * 6,
        out_specs=[VM] * 6,
        out_shape=[
            jax.ShapeDtypeStruct((2 * pairs * GROUPS, ROWS, GW), BF16),
            jax.ShapeDtypeStruct((3 * GROUPS, ROWS, GW), BF16),
            jax.ShapeDtypeStruct((ROWS, GW), BF16),
            jax.ShapeDtypeStruct((D, 2 * D), F32),
            jax.ShapeDtypeStruct((2 * pairs * QP, D), F32),
            jax.ShapeDtypeStruct((pairs, GW), F32),
        ],
        scratch_shapes=[
            pltpu.VMEM((LP, 2 * D), BF16),
            pltpu.VMEM((pairs * LX, 2 * D), BF16),
            pltpu.VMEM((D, pairs * LX), BF16),
        ],
        compiler_params=pltpu.CompilerParams(vmem_limit_bytes=LIMIT),
    )(tangent, text, far_text, query_weight, images, kv_weight, head)


def negative_pairs(picks, tangent, spot, made, kv_weight, head, dq, lrow, grad, arrived, rings, phase):
    last = phase == 2
    pairs = picks.shape[0]
    blocks = tuple(arrived)
    lrow_shape = jax.ShapeDtypeStruct(lrow.shape, F32)
    own_rows = dq.shape[0] // 2
    if last:
        in_hbm = 2
        out_shape = [
            jax.ShapeDtypeStruct((D, D), F32),
            jax.ShapeDtypeStruct((D, D), F32),
            jax.ShapeDtypeStruct((own_rows, D), F32),
            jax.ShapeDtypeStruct((own_rows + pairs // 2, D), F32),
            lrow_shape,
        ]
    else:
        in_hbm = 1
        out_shape = [
            jax.ShapeDtypeStruct(grad.shape, F32), jax.ShapeDtypeStruct(dq.shape, F32), lrow_shape
        ]
    return pl.pallas_call(
        functools.partial(negatives_kernel, pairs=pairs, rings=rings, blocks=blocks, phase=phase),
        in_specs=[SM] * 3 + [VM] * 7 + [ANY] * (1 + len(blocks)),
        out_specs=[ANY] * in_hbm + [VM] * (len(out_shape) - in_hbm),
        out_shape=out_shape,
        scratch_shapes=[
            pltpu.VMEM((LP, 2 * D), BF16),
            pltpu.VMEM((pairs * LX, 2 * D), BF16),
            pltpu.VMEM((pairs, D, LX), BF16),
            pltpu.VMEM((pairs, LP, D), BF16),
            pltpu.VMEM((D, 2 * D), F32),
            pltpu.VMEM((2, D, D) if last else (2, 8, 128), F32),
            pltpu.SMEM((pairs + 1,), jnp.int32),
            pltpu.SemaphoreType.DMA((pairs + 1,)),
            pltpu.SemaphoreType.DMA(()),
            pltpu.SemaphoreType.DMA((4,)),
        ]
        + ([pltpu.VMEM(dq.shape, F32)] if last else []),
        compiler_params=pltpu.CompilerParams(vmem_limit_bytes=LIMIT),
    )(picks, tangent, spot, *made, kv_weight, head, dq, lrow, grad, *arrived.values())


def query_gradient(spot, text, dq, got, rings):
    return pl.pallas_call(
        functools.partial(query_kernel, rings=rings),
        name="query_gradient",
        in_specs=[SM] + [VM] * 3,
        out_specs=[ANY] * 2,
        out_shape=[jax.ShapeDtypeStruct((D // 2, D), F32)] * 2,
        scratch_shapes=[
            pltpu.VMEM((D, D), F32),
            pltpu.VMEM((2, D // 2, D), F32),
            pltpu.SemaphoreType.DMA((2,)),
        ],
        compiler_params=pltpu.CompilerParams(vmem_limit_bytes=LIMIT),
    )(spot, text, dq, got)


def shift(x, axis, step):
    n = lax.axis_size(axis)
    return lax.ppermute(x, axis, [(k, (k + step) % n) for k in range(n)])


AXES = (("dev_1", "dev_0"), ("dev_0", "dev_1"))


def first_steps(images):
    blocks = []
    for color, (near, _) in enumerate(AXES):
        own = images[2 * color : 2 * color + 2]
        blocks.append((own, shift(own, near, 1), shift(own, near, -1)))
    return blocks


def swapped(x):
    return lax.ppermute(x, "dev_2", [(0, 1), (1, 0)])


def next_steps(first):
    soon, then = {}, {}
    for color, (near, far) in enumerate(AXES):
        own, left, right = first[color]
        left_far, right_far = shift(left[:1], near, 1), shift(right[1:], near, -1)
        a = jnp.concatenate([own, left])
        b = jnp.concatenate([right, left_far, right_far])
        soon[color * 8] = a
        soon[color * 8 + 1] = b
        soon[color * 8 + 2] = shift(a, far, 1)
        soon[color * 8 + 5] = shift(b, far, -1)
        then[color * 8 + 3] = shift(b, far, 1)
        then[color * 8 + 4] = shift(a, far, -1)
    return soon, then


def last_steps(soon):
    blocks = {}
    for color, (_, far) in enumerate(AXES):
        blocks[color * 8 + 6] = shift(soon[color * 8 + 2], far, 1)
        blocks[color * 8 + 7] = shift(soon[color * 8 + 5], far, -1)
    return blocks


def together(blocks, other):
    keys = sorted(blocks)
    out = lax.optimization_barrier((other, *[blocks[k] for k in keys]))
    return dict(zip(keys, out[1:])), out[0]


def ring_scatter(blocks, axis):
    n = lax.axis_size(axis)
    me = lax.axis_index(axis)
    sent = []
    for step in range(1, n):
        piece = lax.dynamic_index_in_dim(blocks, (me + step) % n, 0, keepdims=False)
        sent.append(lax.ppermute(piece, axis, [(k, (k + step) % n) for k in range(n)]))
    return sent, lax.dynamic_index_in_dim(blocks, me, 0, keepdims=False)


def reduce_gradients(parts, held):
    width = parts[0].shape[1]
    for stage in range(3):
        moved = []
        for ring, axis in enumerate(RINGS):
            colors = [k for k in range(3) if ORDERS[k][stage] == ring]
            if not colors:
                continue
            n = lax.axis_size(axis)
            blocks = [parts[k].reshape(n, parts[k].shape[0] // n, width) for k in colors]
            rows = blocks[0].shape[1]
            moved.append((colors, rows, ring_scatter(jnp.concatenate(blocks, axis=1), axis)))
        for colors, rows, (sent, kept) in moved:
            for piece in sent:
                kept = kept + piece
            for place, k in enumerate(colors):
                parts[k] = kept[place * rows : (place + 1) * rows]
        if stage == 0:
            parts[2], *held = lax.optimization_barrier((parts[2], *held))
    return parts, held


def local(image_tokens, text_tokens, negatives, query_weight, kv_weight, match_head, cotangent):
    pairs, text_len, model = text_tokens.shape
    images = jnp.pad(image_tokens, ((0, 0), (0, LP - LI), (0, 0)))
    notes = jnp.concatenate([cotangent, negatives.astype(BF16)], axis=1)
    notes = jnp.pad(notes[:, None, :], ((0, 0), (0, QP - LT - 1), (0, model - notes.shape[1])))
    far_text = swapped(jnp.concatenate([text_tokens, notes], axis=1))
    far_notes = far_text[:, LT, : cotangent.shape[1] + negatives.shape[1]]
    first = first_steps(images)
    text = jnp.pad(text_tokens, ((0, 0), (0, QP - LT), (0, 0))).reshape(pairs * QP, model)
    both = jnp.concatenate([cotangent, far_notes[:, : cotangent.shape[1]]], axis=0)
    scale = both.astype(F32) / text_len
    head = match_head.reshape(1, model)
    *made, grad, dq, own_rows = own_pairs(
        scale[:pairs, 0], text, far_text.reshape(pairs * QP, model), query_weight, images, kv_weight, head
    )
    soon, then = next_steps(first)
    passed, dq = together({k: v for k, v in soon.items() if k % 8 in (2, 5)}, dq)
    soon |= passed
    far_blocks = last_steps(soon)
    spot = jnp.stack([lax.axis_index(axis) for axis in DEV]).astype(jnp.int32)
    rings = tuple(lax.axis_size(ring) for ring in RINGS)
    far_negatives = far_notes[:, cotangent.shape[1] :].astype(jnp.int32)
    picks = jnp.concatenate([negatives, far_negatives], axis=0).reshape(-1)
    far_scale = scale[:, 1:].reshape(-1)
    rows = jnp.zeros((picks.shape[0], GW), F32)
    grad, dq, rows = negative_pairs(
        picks, far_scale, spot, made, kv_weight, head, dq, rows, grad, soon, rings, 0
    )
    then, dq = together(then, dq)
    grad, dq, rows = negative_pairs(
        picks, far_scale, spot, made, kv_weight, head, dq, rows, grad, then, rings, 1
    )
    mine, other, dq, give, rows = negative_pairs(
        picks, far_scale, spot, made, kv_weight, head, dq, rows, grad, far_blocks, rings, 2
    )
    got = swapped(give)
    from_core = swapped(other)
    rest = mine.shape[0] // 2
    key_part, value_part, got = lax.optimization_barrier(
        (mine[:rest] + from_core[:rest], mine[rest:] + from_core[rest:], got)
    )
    mine_query, other_query = query_gradient(spot, text, dq, got, rings)
    parts = [mine_query + swapped(other_query), key_part, value_part]
    (grad_query, grad_key, grad_value), (rows, got) = reduce_gradients(parts, (rows, got))
    half = picks.shape[0] // 2
    rows = rows[:half] + got[pairs * QP :, :GW]
    own_logits = jnp.sum(own_rows, axis=1, keepdims=True)
    far_logits = jnp.sum(rows, axis=1).reshape(pairs, 2)
    logits = jnp.concatenate([own_logits, far_logits], axis=1) / text_len
    return logits, grad_query, jnp.concatenate([grad_key, grad_value], axis=1)


def solution(mesh):
    torus = Mesh(
        mesh.devices.reshape(mesh.shape["grp"], 4, 4, 2), ("grp", "dev_0", "dev_1", "dev_2")
    )
    placed = (
        P(GRP_DEV, None, None),
        P(GRP_DEV, None, None),
        P(GRP_DEV, None),
        P(),
        P(),
        P(),
        P(GRP_DEV, None),
    )
    return jax.shard_map(
        local,
        mesh=torus,
        in_specs=placed,
        out_specs=(P(GRP_DEV, None), P(GRP_DEV, None), P(GRP_DEV, None)),
        check_vma=False,
    )
```

```python
import functools

import jax
import jax.numpy as jnp
from jax import lax
from jax.experimental import pallas as pl
from jax.experimental.pallas import tpu as pltpu
from jax.sharding import Mesh
from jax.sharding import PartitionSpec as P


DEV = ("dev_0", "dev_1", "dev_2")
GRP_DEV = ("grp", "dev_0", "dev_1", "dev_2")
RINGS = ("grp", "dev_0", "dev_1")
ORDERS = ((0, 2, 1), (1, 2, 0), (2, 1, 0))

D = 768
LI = 197
LP = 200
LX = 256
LT = 30
QP = 32
GROUPS = 3
GW = 256
ROWS = 128
F32 = jnp.float32
BF16 = jnp.bfloat16


def nn(a, b):
    return lax.dot_general(a, b, (((1,), (0,)), ((), ())), preferred_element_type=F32)


def nt(a, b):
    return lax.dot_general(a, b, (((1,), (1,)), ((), ())), preferred_element_type=F32)


def tn(a, b):
    return lax.dot_general(a, b, (((0,), (0,)), ((), ())), preferred_element_type=F32)


def block_mask():
    row = lax.broadcasted_iota(jnp.int32, (ROWS, GW), 0)
    col = lax.broadcasted_iota(jnp.int32, (ROWS, GW), 1)
    return row, (row // QP) == (col // 64)


def fill_constants(head_ref, mhx_ref, ones_ref):
    row, same = block_mask()
    ones_ref[...] = jnp.where(same & (row % QP < LT), 1.0, 0.0).astype(BF16)
    for g in range(GROUPS):
        rest = head_ref[:, g * GW : (g + 1) * GW]
        for piece in range(3):
            part = rest.astype(BF16)
            rest = rest - part.astype(F32)
            wide = jnp.broadcast_to(part.astype(F32), (ROWS, GW))
            mhx_ref[piece * GROUPS + g] = jnp.where(same, wide, 0.0).astype(BF16)


def attend_pair(i, row, text, scale, keyval, qx_ref, head_ref, mhx_ref, ones_ref, dkv_ref, dq_ref, lrow_ref):
    tail = lax.broadcasted_iota(jnp.int32, (8, ROWS), 0) < (LI - (LP - 8))
    base = pl.multiple_of(i * LX, LX)
    trow = pl.multiple_of(text * QP, QP)
    total = jnp.zeros((1, GW), F32)
    for g in range(GROUPS):
        lo = g * GW
        keys = keyval(lo)
        values = keyval(D + lo)
        query = qx_ref[text * GROUPS + g]
        head = head_ref[:, lo : lo + GW]
        scores = nt(keys, query)
        scores = jnp.concatenate(
            [scores[: LP - 8], jnp.where(tail, scores[LP - 8 :], -1e30)], axis=0
        )
        top = jnp.max(scores, axis=0, keepdims=True)
        expd = jnp.exp(scores - top)
        probs = expd * (1.0 / jnp.sum(expd, axis=0, keepdims=True))
        probs_low = probs.astype(BF16)
        dp = nt(values, mhx_ref[g]) + nt(values, mhx_ref[GROUPS + g]) + nt(values, mhx_ref[2 * GROUPS + g])
        dp = dp * scale
        mean = jnp.sum(probs * dp, axis=0, keepdims=True)
        d_low = (probs * (dp - mean)).astype(BF16)
        dkv_ref[pl.ds(base, LP), lo : lo + GW] = nn(d_low, query).astype(BF16)
        weight = nn(probs_low, ones_ref[...])
        dkv_ref[pl.ds(base, LP), D + lo : D + lo + GW] = (weight * (head * scale)).astype(BF16)
        total = total + jnp.sum(weight * values.astype(F32), axis=0, keepdims=True) * head
        wide = tn(d_low, keys)
        col = lax.broadcasted_iota(jnp.int32, (QP, GW), 1) // 64
        dq = jnp.where(col == 0, wide[:QP], 0.0)
        for h in range(1, 4):
            dq = jnp.where(col == h, wide[h * QP : (h + 1) * QP], dq)
        dq_ref[pl.ds(trow, QP), lo : lo + GW] += dq * 0.125
    lrow_ref[pl.ds(row, 1), :] = total


def own_kernel(
    tan_ref, text_ref, far_text_ref, qw_ref, image_ref, kvw_ref, head_ref,
    qx_ref, mhx_ref, ones_ref, grad_ref, dq_ref, lrow_ref,
    kv_ref, dkv_ref, xt_ref,
    *, pairs,
):
    fill_constants(head_ref, mhx_ref, ones_ref)
    dq_ref[...] = jnp.zeros_like(dq_ref)
    dkv_ref[...] = jnp.zeros_like(dkv_ref)
    _, same = block_mask()
    real = lax.broadcasted_iota(jnp.int32, (pairs * QP, D), 0) % QP < LT
    for side, tokens in enumerate((text_ref, far_text_ref)):
        queries = nn(tokens[...], qw_ref[...]).astype(BF16).astype(F32) * 0.125
        queries = jnp.where(real, queries, 0.0)
        for t in range(pairs):
            for g in range(GROUPS):
                part = queries[t * QP : (t + 1) * QP, g * GW : (g + 1) * GW]
                wide = jnp.concatenate([part] * 4, axis=0)
                qx_ref[(side * pairs + t) * GROUPS + g] = jnp.where(same, wide, 0.0).astype(BF16)

    def one(i, carry):
        image = image_ref[i]
        kv_ref[...] = nn(image, kvw_ref[...]).astype(BF16)
        wide = jnp.concatenate([image, jnp.zeros((LX - LP, D), BF16)], axis=0)
        xt_ref[:, pl.ds(pl.multiple_of(i * LX, LX), LX)] = wide.T
        attend_pair(
            i, i, i, tan_ref[i], lambda lo: kv_ref[:, lo : lo + GW],
            qx_ref, head_ref, mhx_ref, ones_ref, dkv_ref, dq_ref, lrow_ref,
        )
        return carry

    lax.fori_loop(0, pairs, one, 0)

    def block(n, carry):
        cols = pl.ds(pl.multiple_of(n * GW, GW), GW)
        grad_ref[:, cols] = nn(xt_ref[...], dkv_ref[:, cols])
        return carry

    lax.fori_loop(0, 2 * D // GW, block, 0)


def strip_rows(color, rings):
    strips = []
    size = D // (rings[0] * rings[1] * rings[2] * 2)
    for a in range(rings[0]):
        for b in range(rings[1]):
            for c in range(rings[2]):
                at = (a, b, c)
                order = ORDERS[color]
                place = 0
                for ring in order:
                    place = place * rings[ring] + at[ring]
                for core in range(2):
                    source = (((a * rings[1] + b) * rings[2] + c) * 2 + core) * size
                    strips.append((core, source, place * size))
    return size, strips


def locate(negative, spot, rings):
    per_device = 4
    owner = negative // per_device
    inner = negative % per_device
    y_size = rings[2]
    z_off = (owner // (2 * y_size) - spot[0] + rings[1]) % rings[1]
    y_off = ((owner // 2) % y_size - spot[1] + y_size) % y_size
    color = inner // 2
    near = jnp.where(color == 0, y_off, z_off)
    far = jnp.where(color == 0, z_off, y_off)
    half = jnp.where((near == 0) | (near == 3), 0, 1)
    row = inner % 2 + jnp.where((near == 2) | (near == 3), 2, 0)
    kind = jnp.where(far == 0, 0, jnp.where(far == 3, 1, jnp.where(far == 1, 2, 3)))
    number = kind * 2 + half
    phase = jnp.where(kind == 3, 2, jnp.where((number == 3) | (number == 4), 1, 0))
    phase = jnp.where(owner % 2 == spot[2], phase, 3)
    return color * 8 + number, row, phase


def negatives_kernel(
    pick_ref, tan_ref, spot_ref, qx_ref, mhx_ref, ones_ref, kvw_ref, head_ref, dq_in_ref, lrow_in_ref,
    grad_in_ref, *rest,
    pairs, rings, blocks, phase,
):
    last = phase == 2
    pieces, rest = rest[: len(blocks)], rest[len(blocks) :]
    if last:
        mine_ref, other_ref, own_dq_ref, give_ref, lrow_ref = rest[:5]
        rest = rest[5:]
    else:
        out_grad_ref, dq_ref, lrow_ref = rest[:3]
        rest = rest[3:] + (dq_ref,)
    kv_ref, dkv_ref, xt_ref, image_ref, prior_ref, out_ref, list_ref, sems, prior_sem, out_sems, dq_ref = rest
    spot = [spot_ref[k] for k in range(3)]
    count = jnp.int32(0)
    for j in range(pairs):
        block, row, when = locate(pick_ref[j], spot, rings)
        here = when == phase
        list_ref[count] = j
        for k, piece in enumerate(pieces):

            @pl.when(here & (block == blocks[k]))
            def _():
                pltpu.make_async_copy(piece.at[row], image_ref.at[count], sems.at[count]).start()

        count = count + here.astype(jnp.int32)
    prior = pltpu.make_async_copy(grad_in_ref, prior_ref, prior_sem)
    prior.start()
    dq_ref[...] = dq_in_ref[...]
    lrow_ref[...] = lrow_in_ref[...]

    def one(i, carry):
        dkv_ref[pl.ds(pl.multiple_of(i * LX + LP - 8, 64), LX - LP + 8), :] = jnp.zeros((LX - LP + 8, 2 * D), BF16)
        pltpu.make_async_copy(pieces[0].at[0], image_ref.at[i], sems.at[i]).wait()
        j = list_ref[i]
        image = image_ref[i]
        kv_ref[...] = nn(image, kvw_ref[...]).astype(BF16)
        wide = jnp.concatenate([image, jnp.zeros((LX - LP, D), BF16)], axis=0)
        xt_ref[i] = wide.T
        attend_pair(
            i, j, j // 2, tan_ref[j], lambda lo: kv_ref[:, lo : lo + GW],
            qx_ref, head_ref, mhx_ref, ones_ref, dkv_ref, dq_ref, lrow_ref,
        )
        return carry

    lax.fori_loop(0, count, one, 0)
    twos = (count + 1) // 2

    @pl.when(count % 2 == 1)
    def _():
        dkv_ref[pl.ds(pl.multiple_of(count * LX, LX), LX), :] = jnp.zeros((LX, 2 * D), BF16)
        xt_ref[count] = jnp.zeros((D, LX), BF16)

    def products(part):
        def two(k, carry):
            left = xt_ref[2 * k]
            right = xt_ref[2 * k + 1]
            rows = pl.ds(pl.multiple_of(2 * k * LX, LX), LX)
            more = pl.ds(pl.multiple_of((2 * k + 1) * LX, LX), LX)

            def cols(n, inner):
                at = pl.ds(pl.multiple_of(n * GW, GW), GW)
                wide = pl.ds(pl.multiple_of(part * D + n * GW, GW), GW)
                prior_ref[:, wide] += nn(left, dkv_ref[rows, wide]) + nn(right, dkv_ref[more, wide])
                return inner

            return lax.fori_loop(0, D // GW, cols, carry)

        lax.fori_loop(0, twos, two, 0)

    prior.wait()
    if not last:
        copies = []
        for part in range(2):
            products(part)
            cols = pl.ds(part * D, D)
            copies.append(
                pltpu.make_async_copy(prior_ref.at[:, cols], out_grad_ref.at[:, cols], out_sems.at[part])
            )
            copies[-1].start()
    else:
        rows = own_dq_ref.shape[0]
        own_dq_ref[...] = dq_ref[:rows]
        give_ref[:rows] = dq_ref[rows:]
        give_ref[rows:] = jnp.zeros((pairs // 2, D), F32)
        give_ref[rows:, :GW] = lrow_ref[pairs // 2 :]
        copies = []
        for part in range(2):
            products(part)
            copies += spread(part + 1, part, prior_ref, part * D, out_ref, mine_ref, other_ref, out_sems, spot[2], rings)
    for copy in copies:
        copy.wait()


def spread(color, place, source_ref, lo, out_ref, mine_ref, other_ref, sems, core, rings):
    half = D // 2
    size, strips = strip_rows(color, rings)
    for which, source, target in strips:
        slot = jnp.where(core == which, 0, 1)
        out_ref[slot, place * half + target : place * half + target + size, :] = source_ref[
            source : source + size, lo : lo + D
        ]
    copies = []
    for slot, ref in ((1, other_ref), (0, mine_ref)):
        copy = pltpu.make_async_copy(
            out_ref.at[slot, pl.ds(place * half, half)],
            ref.at[pl.ds(place * half, half)],
            sems.at[2 * place + slot],
        )
        copy.start()
        copies.append(copy)
    return copies


def query_kernel(
    spot_ref, text_ref, dq_ref, got_ref, mine_ref, other_ref, grad_ref, out_ref, sems, *, rings
):
    rows = text_ref.shape[0]
    total = dq_ref[:rows] + got_ref[:rows]
    grad_ref[...] = tn(text_ref[...], total.astype(BF16))
    for copy in spread(0, 0, grad_ref, 0, out_ref, mine_ref, other_ref, sems, spot_ref[2], rings):
        copy.wait()


VM = pl.BlockSpec(memory_space=pltpu.VMEM)
SM = pl.BlockSpec(memory_space=pltpu.SMEM)
ANY = pl.BlockSpec(memory_space=pl.ANY)
LIMIT = 60 * 1024 * 1024


def own_pairs(tangent, text, far_text, query_weight, images, kv_weight, head):
    pairs = images.shape[0]
    return pl.pallas_call(
        functools.partial(own_kernel, pairs=pairs),
        name="own_pairs",
        in_specs=[SM] + [VM] * 6,
        out_specs=[VM] * 6,
        out_shape=[
            jax.ShapeDtypeStruct((2 * pairs * GROUPS, ROWS, GW), BF16),
            jax.ShapeDtypeStruct((3 * GROUPS, ROWS, GW), BF16),
            jax.ShapeDtypeStruct((ROWS, GW), BF16),
            jax.ShapeDtypeStruct((D, 2 * D), F32),
            jax.ShapeDtypeStruct((2 * pairs * QP, D), F32),
            jax.ShapeDtypeStruct((pairs, GW), F32),
        ],
        scratch_shapes=[
            pltpu.VMEM((LP, 2 * D), BF16),
            pltpu.VMEM((pairs * LX, 2 * D), BF16),
            pltpu.VMEM((D, pairs * LX), BF16),
        ],
        compiler_params=pltpu.CompilerParams(vmem_limit_bytes=LIMIT),
    )(tangent, text, far_text, query_weight, images, kv_weight, head)


def negative_pairs(picks, tangent, spot, made, kv_weight, head, dq, lrow, grad, arrived, rings, phase):
    last = phase == 2
    pairs = picks.shape[0]
    blocks = tuple(arrived)
    lrow_shape = jax.ShapeDtypeStruct(lrow.shape, F32)
    own_rows = dq.shape[0] // 2
    if last:
        in_hbm = 2
        out_shape = [
            jax.ShapeDtypeStruct((D, D), F32),
            jax.ShapeDtypeStruct((D, D), F32),
            jax.ShapeDtypeStruct((own_rows, D), F32),
            jax.ShapeDtypeStruct((own_rows + pairs // 2, D), F32),
            lrow_shape,
        ]
    else:
        in_hbm = 1
        out_shape = [
            jax.ShapeDtypeStruct(grad.shape, F32), jax.ShapeDtypeStruct(dq.shape, F32), lrow_shape
        ]
    return pl.pallas_call(
        functools.partial(negatives_kernel, pairs=pairs, rings=rings, blocks=blocks, phase=phase),
        in_specs=[SM] * 3 + [VM] * 7 + [ANY] * (1 + len(blocks)),
        out_specs=[ANY] * in_hbm + [VM] * (len(out_shape) - in_hbm),
        out_shape=out_shape,
        scratch_shapes=[
            pltpu.VMEM((LP, 2 * D), BF16),
            pltpu.VMEM((pairs * LX, 2 * D), BF16),
            pltpu.VMEM((pairs, D, LX), BF16),
            pltpu.VMEM((pairs, LP, D), BF16),
            pltpu.VMEM((D, 2 * D), F32),
            pltpu.VMEM((2, D, D) if last else (2, 8, 128), F32),
            pltpu.SMEM((pairs + 1,), jnp.int32),
            pltpu.SemaphoreType.DMA((pairs + 1,)),
            pltpu.SemaphoreType.DMA(()),
            pltpu.SemaphoreType.DMA((4,)),
        ]
        + ([pltpu.VMEM(dq.shape, F32)] if last else []),
        compiler_params=pltpu.CompilerParams(vmem_limit_bytes=LIMIT),
    )(picks, tangent, spot, *made, kv_weight, head, dq, lrow, grad, *arrived.values())


def query_gradient(spot, text, dq, got, rings):
    return pl.pallas_call(
        functools.partial(query_kernel, rings=rings),
        name="query_gradient",
        in_specs=[SM] + [VM] * 3,
        out_specs=[ANY] * 2,
        out_shape=[jax.ShapeDtypeStruct((D // 2, D), F32)] * 2,
        scratch_shapes=[
            pltpu.VMEM((D, D), F32),
            pltpu.VMEM((2, D // 2, D), F32),
            pltpu.SemaphoreType.DMA((2,)),
        ],
        compiler_params=pltpu.CompilerParams(vmem_limit_bytes=LIMIT),
    )(spot, text, dq, got)


def shift(x, axis, step):
    n = lax.axis_size(axis)
    return lax.ppermute(x, axis, [(k, (k + step) % n) for k in range(n)])


AXES = (("dev_1", "dev_0"), ("dev_0", "dev_1"))


def first_steps(images):
    blocks = []
    for color, (near, _) in enumerate(AXES):
        own = images[2 * color : 2 * color + 2]
        blocks.append((own, shift(own, near, 1), shift(own, near, -1)))
    return blocks


def swapped(x):
    return lax.ppermute(x, "dev_2", [(0, 1), (1, 0)])


def next_steps(first):
    soon, then = {}, {}
    for color, (near, far) in enumerate(AXES):
        own, left, right = first[color]
        left_far, right_far = shift(left[:1], near, 1), shift(right[1:], near, -1)
        a = jnp.concatenate([own, left])
        b = jnp.concatenate([right, left_far, right_far])
        soon[color * 8] = a
        soon[color * 8 + 1] = b
        soon[color * 8 + 2] = shift(a, far, 1)
        soon[color * 8 + 5] = shift(b, far, -1)
        then[color * 8 + 3] = shift(b, far, 1)
        then[color * 8 + 4] = shift(a, far, -1)
    return soon, then


def last_steps(soon):
    blocks = {}
    for color, (_, far) in enumerate(AXES):
        blocks[color * 8 + 6] = shift(soon[color * 8 + 2], far, 1)
        blocks[color * 8 + 7] = shift(soon[color * 8 + 5], far, -1)
    return blocks


def together(blocks, other):
    keys = sorted(blocks)
    out = lax.optimization_barrier((other, *[blocks[k] for k in keys]))
    return dict(zip(keys, out[1:])), out[0]


def ring_scatter(blocks, axis):
    n = lax.axis_size(axis)
    me = lax.axis_index(axis)
    sent = []
    for step in range(1, n):
        piece = lax.dynamic_index_in_dim(blocks, (me + step) % n, 0, keepdims=False)
        sent.append(lax.ppermute(piece, axis, [(k, (k + step) % n) for k in range(n)]))
    return sent, lax.dynamic_index_in_dim(blocks, me, 0, keepdims=False)


def reduce_gradients(parts, held):
    width = parts[0].shape[1]
    for stage in range(3):
        moved = []
        for ring, axis in enumerate(RINGS):
            colors = [k for k in range(3) if ORDERS[k][stage] == ring]
            if not colors:
                continue
            n = lax.axis_size(axis)
            blocks = [parts[k].reshape(n, parts[k].shape[0] // n, width) for k in colors]
            rows = blocks[0].shape[1]
            moved.append((colors, rows, ring_scatter(jnp.concatenate(blocks, axis=1), axis)))
        for colors, rows, (sent, kept) in moved:
            for piece in sent:
                kept = kept + piece
            for place, k in enumerate(colors):
                parts[k] = kept[place * rows : (place + 1) * rows]
        if stage == 0:
            parts[2], *held = lax.optimization_barrier((parts[2], *held))
    return parts, held


def local(image_tokens, text_tokens, negatives, query_weight, kv_weight, match_head, cotangent):
    pairs, text_len, model = text_tokens.shape
    images = jnp.pad(image_tokens, ((0, 0), (0, LP - LI), (0, 0)))
    notes = jnp.concatenate([cotangent, negatives.astype(BF16)], axis=1)
    notes = jnp.pad(notes[:, None, :], ((0, 0), (0, QP - LT - 1), (0, model - notes.shape[1])))
    far_text = swapped(jnp.concatenate([text_tokens, notes], axis=1))
    far_notes = far_text[:, LT, : cotangent.shape[1] + negatives.shape[1]]
    first = first_steps(images)
    text = jnp.pad(text_tokens, ((0, 0), (0, QP - LT), (0, 0))).reshape(pairs * QP, model)
    both = jnp.concatenate([cotangent, far_notes[:, : cotangent.shape[1]]], axis=0)
    scale = both.astype(F32) / text_len
    head = match_head.reshape(1, model)
    *made, grad, dq, own_rows = own_pairs(
        scale[:pairs, 0], text, far_text.reshape(pairs * QP, model), query_weight, images, kv_weight, head
    )
    soon, then = next_steps(first)
    passed, dq = together({k: v for k, v in soon.items() if k % 8 in (2, 5)}, dq)
    soon |= passed
    far_blocks = last_steps(soon)
    spot = jnp.stack([lax.axis_index(axis) for axis in DEV]).astype(jnp.int32)
    rings = tuple(lax.axis_size(ring) for ring in RINGS)
    far_negatives = far_notes[:, cotangent.shape[1] :].astype(jnp.int32)
    picks = jnp.concatenate([negatives, far_negatives], axis=0).reshape(-1)
    far_scale = scale[:, 1:].reshape(-1)
    rows = jnp.zeros((picks.shape[0], GW), F32)
    grad, dq, rows = negative_pairs(
        picks, far_scale, spot, made, kv_weight, head, dq, rows, grad, soon, rings, 0
    )
    then, dq = together(then, dq)
    grad, dq, rows = negative_pairs(
        picks, far_scale, spot, made, kv_weight, head, dq, rows, grad, then, rings, 1
    )
    mine, other, dq, give, rows = negative_pairs(
        picks, far_scale, spot, made, kv_weight, head, dq, rows, grad, far_blocks, rings, 2
    )
    got = swapped(give)
    from_core = swapped(other)
    mine_query, other_query = query_gradient(spot, text, dq, got, rings)
    rest = mine.shape[0] // 2
    parts = [mine_query + swapped(other_query), mine[:rest] + from_core[:rest], mine[rest:] + from_core[rest:]]
    (grad_query, grad_key, grad_value), (rows, got) = reduce_gradients(parts, (rows, got))
    half = picks.shape[0] // 2
    rows = rows[:half] + got[pairs * QP :, :GW]
    own_logits = jnp.sum(own_rows, axis=1, keepdims=True)
    far_logits = jnp.sum(rows, axis=1).reshape(pairs, 2)
    logits = jnp.concatenate([own_logits, far_logits], axis=1) / text_len
    return logits, grad_query, jnp.concatenate([grad_key, grad_value], axis=1)


def solution(mesh):
    torus = Mesh(
        mesh.devices.reshape(mesh.shape["grp"], 4, 4, 2), ("grp", "dev_0", "dev_1", "dev_2")
    )
    placed = (
        P(GRP_DEV, None, None),
        P(GRP_DEV, None, None),
        P(GRP_DEV, None),
        P(),
        P(),
        P(),
        P(GRP_DEV, None),
    )
    return jax.shard_map(
        local,
        mesh=torus,
        in_specs=placed,
        out_specs=(P(GRP_DEV, None), P(GRP_DEV, None), P(GRP_DEV, None)),
        check_vma=False,
    )
```
